32 devices in a mesh: rep: 8 (over z, x), shard: 4 (over y, core).
Axes of the slice: x: 2, y: 2, z: 4, core: 2. Of those that a mesh axis runs over, the one named last changes fastest.
Arguments:
- latents: bfloat16 [128, 256, 384], P(('rep', 'shard')), may hold values from -6 to 6
- cotangent: bfloat16 [128, 256, 384], P(('rep', 'shard'))
- counts: int32 [32], P(('rep', 'shard')), may hold values from 3 to 4, as said below
- labels: int32 [128], P(('rep', 'shard')), may hold values from 0 to 999
- timesteps: int32 [128], P(('rep', 'shard')), may hold values from 0 to 999
- class_table: bfloat16 [1000, 384], replicated, may hold values from -6 to 6
- ada_weight: bfloat16 [384, 2304], P('shard'), may hold values from -0.3125 to 0.3125
- ada_bias: bfloat16 [2304], P('shard'), may hold values from -3 to 3
- qkv_weight: bfloat16 [384, 1152], P('shard')
- query_bias: bfloat16 [384], P('shard'), may hold values from -3 to 3
- value_bias: bfloat16 [384], P('shard'), may hold values from -3 to 3
- proj_weight: bfloat16 [384, 384], P('shard'), may hold values from -1.25 to 1.25
- proj_bias: bfloat16 [384], P('shard'), may hold values from -3 to 3
- hidden_weight: bfloat16 [384, 1536], P('shard'), may hold values from -0.3125 to 0.3125
- hidden_bias: bfloat16 [1536], P('shard'), may hold values from -3 to 3
- output_weight: bfloat16 [1536, 384], P('shard'), may hold values from -0.15625 to 0.15625
- output_bias: bfloat16 [384], P('shard'), may hold values from -3 to 3
Outputs:
- block_output: bfloat16 [128, 256, 384], P(('rep', 'shard'))
- grad_input: float32 [128, 256, 384], P(('rep', 'shard'))
- grad_cond: float32 [128, 384], P(('rep', 'shard'))
- grad_ada_weight: float32 [384, 2304], P('shard')
- grad_ada_bias: float32 [2304], P('shard')
- grad_qkv_weight: float32 [384, 1152], P('shard')
- grad_query_bias: float32 [384], P('shard')
- grad_value_bias: float32 [384], P('shard')
- grad_proj_weight: float32 [384, 384], P('shard')
- grad_proj_bias: float32 [384], P('shard')
- grad_hidden_weight: float32 [384, 1536], P('shard')
- grad_hidden_bias: float32 [1536], P('shard')
- grad_output_weight: float32 [1536, 384], P('shard')
- grad_output_bias: float32 [384], P('shard')
The draws below stay inside these ranges and needn't reach their ends.
Inputs may be any that keep to these rules, and one draw needn't show every extreme that they name: `counts`: every device holds 3 or 4 live latents, its first slots; both occur.
All inputs are finite; a program needn't handle non-finite values.
Results may differ from the reference program's by a relative error of at most 0.02.
The reference program's roundings to bfloat16 on the way (of `silu_cond`, `attn_in`, `probs`, `mixed_heads`, `mlp_in`, `hidden_act`, `d_mixed` and `d_scores`) count: a program that leaves them out, or rounds other values in their place, can miss the bound.
Values may be sent and summed in bfloat16 or wider, within the bound.
No kernel may reach another device: no remote copies, remote signals or barrier semaphores. Data moves between devices by JAX's collectives and lax.ppermute only.
A program may use at most 128 MiB of HBM per device.

```python
import math
import jax
import jax.numpy as jnp
from jax import lax

D = 384
HEADS = 6
FF = 1536
CLASSES = 1000
TSTEPS = 1000
SEQ = 256
SLOTS = 4
LATENTS = 128
DEVICES = 32


def draw_cotangent(key, part):
    key_vals = jax.random.fold_in(jax.random.fold_in(key, 11), 0)
    ramp = 1.0 + 2.0 * jnp.arange(LATENTS, dtype=jnp.float32) / max(LATENTS - 1, 1)
    entries = jax.random.truncated_normal(key_vals, -4.0, 4.0, (LATENTS, SEQ, D), jnp.float32)
    return (entries * ramp[:, None, None]).astype(jnp.bfloat16)


def draw_counts(key, part):
    key_base, key_order = jax.random.split(jax.random.fold_in(key, 23))
    base_counts = jax.random.randint(key_base, (DEVICES,), SLOTS - 1, SLOTS + 1, jnp.int32)
    order = jax.random.permutation(key_order, DEVICES)
    base_counts = base_counts.at[order[0]].set(SLOTS)
    base_counts = base_counts.at[order[1]].set(SLOTS - 1)
    return base_counts.astype(jnp.int32)


def draw_qkv_weight(key, part):
    key_main = jax.random.fold_in(key, 37)
    spread = D ** (-0.5)
    entries = jax.random.truncated_normal(key_main, -3.0, 3.0, (D, 3 * D), jnp.float32) * spread
    return entries.astype(jnp.bfloat16)


def with_ends(array, rng, smallest, largest):
    longest = array.shape.index(max(array.shape))
    spots = []
    for shift in (0, 1):
        where = [jax.random.randint(jax.random.fold_in(rng, axis), (), 0, length) for axis, length in enumerate(array.shape)]
        where[longest] = (where[longest] + shift) % array.shape[longest]
        spots.append(tuple(where))
    return array.at[spots[0]].set(smallest).at[spots[1]].set(largest)


def steps_of(stream_key, extent, cuts, least, top_value):
    level = 1.0
    for axis_at, blocks in cuts:
        heights = jax.random.uniform(jax.random.fold_in(jax.random.fold_in(stream_key, 6), axis_at), (blocks,), jnp.float32, least / len(cuts), top_value / len(cuts))
        level = level * jnp.repeat(jnp.exp(heights), extent[axis_at] // blocks).reshape((-1,) + (1,) * (len(extent) - 1 - axis_at))
    return level


def normal_values(rng, dims, deviation, most, cuts=(), kind=jnp.bfloat16):
    factor_of = steps_of(rng, dims, cuts, -0.22, 0.18) if cuts else 1.0
    drawn = jax.random.normal(rng, dims, jnp.float32) * deviation * factor_of
    return jnp.minimum(jnp.maximum(drawn, -most), most).astype(kind)


def setup_inputs(seed: int = 0) -> dict:
    keys = jax.random.split(jax.random.key(seed), 18)
    latents = normal_values(keys[0], (LATENTS, SEQ, D), 1.0, 6.0, ((0, 32),))
    cotangent = draw_cotangent(jax.random.fold_in(keys[17], 71), 0)
    counts = draw_counts(jax.random.fold_in(keys[17], 71), 0)
    labels = with_ends(jax.random.randint(keys[3], (LATENTS,), 0, CLASSES), jax.random.fold_in(keys[3], 1), 0, CLASSES - 1).astype(jnp.int32)
    timesteps = with_ends(jax.random.randint(keys[4], (LATENTS,), 0, TSTEPS), jax.random.fold_in(keys[4], 1), 0, TSTEPS - 1).astype(jnp.int32)
    class_table = normal_values(keys[5], (CLASSES, D), 1.0, 6.0)
    ada_weight = normal_values(keys[6], (D, 6 * D), D ** -0.5, 0.3125, ((0, 4),))
    ada_bias = normal_values(keys[7], (6 * D,), 0.5, 3.0, ((0, 4),))
    qkv_weight = draw_qkv_weight(jax.random.fold_in(keys[17], 71), 0)
    query_bias = normal_values(keys[9], (D,), 0.5, 3.0, ((0, 4),))
    value_bias = normal_values(keys[10], (D,), 0.5, 3.0, ((0, 4),))
    proj_weight = normal_values(keys[11], (D, D), (D // 16) ** -0.5, 1.25, ((0, 4),))
    proj_bias = normal_values(keys[12], (D,), 0.5, 3.0, ((0, 4),))
    hidden_weight = normal_values(keys[13], (D, FF), D ** -0.5, 0.3125, ((0, 4),))
    hidden_bias = normal_values(keys[14], (FF,), 0.5, 3.0, ((0, 4),))
    output_weight = normal_values(keys[15], (FF, D), FF ** -0.5, 0.15625, ((0, 4),))
    output_bias = normal_values(keys[16], (D,), 0.5, 3.0, ((0, 4),))
    return dict(latents=latents, cotangent=cotangent, counts=counts, labels=labels, timesteps=timesteps, class_table=class_table, ada_weight=ada_weight, ada_bias=ada_bias, qkv_weight=qkv_weight, query_bias=query_bias, value_bias=value_bias, proj_weight=proj_weight, proj_bias=proj_bias, hidden_weight=hidden_weight, hidden_bias=hidden_bias, output_weight=output_weight, output_bias=output_bias)


EPSILON = 1e-06
GELU_SCALE = math.sqrt(2.0 / math.pi)
GELU_CUBIC = 0.044715

def matmul(left_side, right_side):
    return jnp.dot(left_side, right_side, preferred_element_type=jnp.float32)

def batched(pattern, left_side, right_side):
    return jnp.einsum(pattern, left_side.astype(jnp.float32), right_side.astype(jnp.float32))

def layer_norm(tensor):
    average = lax.optimization_barrier(jnp.mean(tensor, axis=-1, keepdims=True))
    centred = tensor - average
    variance = lax.optimization_barrier(jnp.mean(centred * centred, axis=-1, keepdims=True))
    inv_std = lax.rsqrt(variance + EPSILON)
    return (centred * inv_std, inv_std)

def norm_backward(upstream, normed, inv_std):
    first_mean = lax.optimization_barrier(jnp.mean(upstream, axis=-1, keepdims=True))
    second_mean = lax.optimization_barrier(jnp.mean(upstream * normed, axis=-1, keepdims=True))
    return inv_std * (upstream - first_mean - normed * second_mean)

def gelu_parts(pre_act):
    inner = GELU_SCALE * (pre_act + GELU_CUBIC * pre_act * pre_act * pre_act)
    tanh_val = jnp.tanh(inner)
    result = 0.5 * pre_act * (1.0 + tanh_val)
    slope = 0.5 * (1.0 + tanh_val) + 0.5 * pre_act * (1.0 - tanh_val * tanh_val) * GELU_SCALE * (1.0 + 3.0 * GELU_CUBIC * pre_act * pre_act)
    return (result, slope)

def time_embed(step_ids, model_width):
    half_width = model_width // 2
    frequency = jnp.exp(-math.log(10000.0) * jnp.arange(half_width, dtype=jnp.float32) / half_width)
    angles = step_ids.astype(jnp.float32)[:, None] * frequency[None, :]
    return jnp.concatenate([jnp.cos(angles), jnp.sin(angles)], axis=1)

def forward_pass(latents, conditioning, live_mask, weights):
    ada_weight, qkv_weight, proj_weight, hidden_weight, output_weight, ada_bias, query_bias, value_bias, proj_bias, hidden_bias, output_bias = weights
    batch_size, seq_len, model_width = latents.shape
    head_size = model_width // HEADS
    row_count = batch_size * seq_len
    scale_factor = head_size ** (-0.5)
    silu_cond = (conditioning * jax.nn.sigmoid(conditioning)).astype(jnp.bfloat16)
    modulation = matmul(silu_cond, ada_weight) + ada_bias.astype(jnp.float32)
    pieces = tuple((modulation[:, None, piece_index * model_width:(piece_index + 1) * model_width] for piece_index in range(6)))
    shift_one, scale_one, gate_one, shift_two, scale_two, gate_two = pieces
    inputs = latents.astype(jnp.float32)
    normed_one, inv_one = layer_norm(inputs)
    attn_in = (normed_one * (1.0 + scale_one) + shift_one).astype(jnp.bfloat16).reshape(row_count, model_width)
    proj_all = matmul(attn_in, qkv_weight)
    head_shape = (batch_size, seq_len, HEADS, head_size)
    queries = (proj_all[:, :model_width] + query_bias.astype(jnp.float32)).astype(jnp.bfloat16).reshape(head_shape)
    key_rows = proj_all[:, model_width:2 * model_width].astype(jnp.bfloat16).reshape(head_shape)
    value_rows = (proj_all[:, 2 * model_width:] + value_bias.astype(jnp.float32)).astype(jnp.bfloat16).reshape(head_shape)
    scores = batched('bqhd,bkhd->bhqk', queries, key_rows) * scale_factor
    top_score = lax.optimization_barrier(jnp.max(scores, axis=-1, keepdims=True))
    log_total = top_score + jnp.log(lax.optimization_barrier(jnp.sum(jnp.exp(scores - top_score), axis=-1, keepdims=True)))
    probs = jnp.exp(scores - log_total).astype(jnp.bfloat16)
    mixed_heads = batched('bhqk,bkhd->bqhd', probs, value_rows).astype(jnp.bfloat16).reshape(row_count, model_width)
    attn_out = (matmul(mixed_heads, proj_weight) + proj_bias.astype(jnp.float32)).reshape(batch_size, seq_len, model_width)
    middle = inputs + gate_one * attn_out
    normed_two, inv_two = layer_norm(middle)
    mlp_in = (normed_two * (1.0 + scale_two) + shift_two).astype(jnp.bfloat16).reshape(row_count, model_width)
    hidden_pre = matmul(mlp_in, hidden_weight) + hidden_bias.astype(jnp.float32)
    hidden_val, hidden_slope = gelu_parts(hidden_pre)
    hidden_act = hidden_val.astype(jnp.bfloat16)
    mlp_out = (matmul(hidden_act, output_weight) + output_bias.astype(jnp.float32)).reshape(batch_size, seq_len, model_width)
    block_output = (live_mask[:, None, None] * (middle + gate_two * mlp_out)).astype(jnp.bfloat16)
    stored = (pieces, silu_cond, normed_one, inv_one, attn_in, queries, key_rows, value_rows, log_total, mixed_heads, attn_out, normed_two, inv_two, mlp_in, hidden_slope, hidden_act, mlp_out)
    return (block_output, stored)

def mlp_backward(cotangent, live_mask, stored, weights):
    ada_weight, qkv_weight, proj_weight, hidden_weight, output_weight = weights[:5]
    pieces, silu_cond, normed_one, inv_one, attn_in, queries, key_rows, value_rows, log_total, mixed_heads, attn_out, normed_two, inv_two, mlp_in, hidden_slope, hidden_act, mlp_out = stored
    shift_one, scale_one, gate_one, shift_two, scale_two, gate_two = pieces
    batch_size, seq_len, model_width = cotangent.shape
    row_count = batch_size * seq_len
    grad_out = live_mask[:, None, None] * cotangent.astype(jnp.float32)
    d_gate_two = lax.optimization_barrier(jnp.sum(grad_out * mlp_out, axis=1))
    d_mlp = (grad_out * gate_two).reshape(row_count, model_width)
    d_mlp_b = d_mlp.astype(jnp.bfloat16)
    grad_output_bias = lax.optimization_barrier(jnp.sum(d_mlp, axis=0))
    grad_output_weight = matmul(hidden_act.T, d_mlp_b)
    d_pre = matmul(d_mlp_b, output_weight.T) * hidden_slope
    d_pre_b = d_pre.astype(jnp.bfloat16)
    grad_hidden_bias = lax.optimization_barrier(jnp.sum(d_pre, axis=0))
    grad_hidden_weight = matmul(mlp_in.T, d_pre_b)
    d_mlp_in = matmul(d_pre_b, hidden_weight.T).reshape(batch_size, seq_len, model_width)
    d_shift_two = lax.optimization_barrier(jnp.sum(d_mlp_in, axis=1))
    d_scale_two = lax.optimization_barrier(jnp.sum(d_mlp_in * normed_two, axis=1))
    d_middle = grad_out + norm_backward(d_mlp_in * (1.0 + scale_two), normed_two, inv_two)
    return ((grad_hidden_weight, grad_output_weight, grad_hidden_bias, grad_output_bias), (d_middle, d_shift_two, d_scale_two, d_gate_two))

def attention_backward(conditioning, stored, weights, mlp_part):
    ada_weight, qkv_weight, proj_weight, hidden_weight, output_weight = weights[:5]
    pieces, silu_cond, normed_one, inv_one, attn_in, queries, key_rows, value_rows, log_total, mixed_heads, attn_out, normed_two, inv_two, mlp_in, hidden_slope, hidden_act, mlp_out = stored
    shift_one, scale_one, gate_one, shift_two, scale_two, gate_two = pieces
    d_middle, d_shift_two, d_scale_two, d_gate_two = mlp_part
    batch_size, seq_len, head_count, head_size = queries.shape
    model_width = head_count * head_size
    row_count = batch_size * seq_len
    scale_factor = head_size ** (-0.5)
    d_gate_one = lax.optimization_barrier(jnp.sum(d_middle * attn_out, axis=1))
    d_attn = (d_middle * gate_one).reshape(row_count, model_width)
    d_attn_b = d_attn.astype(jnp.bfloat16)
    grad_proj_bias = lax.optimization_barrier(jnp.sum(d_attn, axis=0))
    grad_proj_weight = matmul(mixed_heads.T, d_attn_b)
    d_mixed = matmul(d_attn_b, proj_weight.T).astype(jnp.bfloat16).reshape(queries.shape)
    scores = batched('bqhd,bkhd->bhqk', queries, key_rows) * scale_factor
    probs = jnp.exp(scores - log_total)
    probs_b = probs.astype(jnp.bfloat16)
    d_probs = batched('bqhd,bkhd->bhqk', d_mixed, value_rows)
    row_dot = lax.optimization_barrier(jnp.sum(probs * d_probs, axis=-1, keepdims=True))
    d_scores = (probs * (d_probs - row_dot) * scale_factor).astype(jnp.bfloat16)
    d_queries = batched('bhqk,bkhd->bqhd', d_scores, key_rows).reshape(row_count, model_width)
    d_keys = batched('bhqk,bqhd->bkhd', d_scores, queries).reshape(row_count, model_width)
    d_values = batched('bhqk,bqhd->bkhd', probs_b, d_mixed).reshape(row_count, model_width)
    grad_query_bias = lax.optimization_barrier(jnp.sum(d_queries, axis=0))
    grad_value_bias = lax.optimization_barrier(jnp.sum(d_values, axis=0))
    d_proj_all = jnp.concatenate([d_queries, d_keys, d_values], axis=1).astype(jnp.bfloat16)
    grad_qkv_weight = matmul(attn_in.T, d_proj_all)
    d_attn_in = matmul(d_proj_all, qkv_weight.T).reshape(batch_size, seq_len, model_width)
    d_shift_one = lax.optimization_barrier(jnp.sum(d_attn_in, axis=1))
    d_scale_one = lax.optimization_barrier(jnp.sum(d_attn_in * normed_one, axis=1))
    grad_input = d_middle + norm_backward(d_attn_in * (1.0 + scale_one), normed_one, inv_one)
    d_modulation = jnp.concatenate([d_shift_one, d_scale_one, d_gate_one, d_shift_two, d_scale_two, d_gate_two], axis=1)
    d_mod_b = d_modulation.astype(jnp.bfloat16)
    grad_ada_bias = lax.optimization_barrier(jnp.sum(d_modulation, axis=0))
    grad_ada_weight = matmul(silu_cond.T, d_mod_b)
    sig_cond = jax.nn.sigmoid(conditioning)
    grad_cond = matmul(d_mod_b, ada_weight.T) * sig_cond * (1.0 + conditioning * (1.0 - sig_cond))
    return ((grad_ada_weight, grad_qkv_weight, grad_proj_weight, grad_ada_bias, grad_query_bias, grad_value_bias, grad_proj_bias), grad_input, grad_cond)

def reference(latents, cotangent, counts, labels, timesteps, class_table, ada_weight, ada_bias, qkv_weight, query_bias, value_bias, proj_weight, proj_bias, hidden_weight, hidden_bias, output_weight, output_bias):
    weights = (ada_weight, qkv_weight, proj_weight, hidden_weight, output_weight, ada_bias, query_bias, value_bias, proj_bias, hidden_bias, output_bias)
    latent_count = latents.shape[0]
    group_size = math.gcd(latent_count, max(1, 4096 // SEQ))
    step_total = latent_count // group_size
    positions = jnp.arange(latent_count, dtype=jnp.int32)
    owners = (positions // SLOTS).astype(jnp.int32)
    live_mask = (positions % SLOTS < counts[owners]).astype(jnp.float32)
    conditioning = class_table[labels].astype(jnp.float32) + time_embed(timesteps, D)

    def shaped(tensor):
        return tensor.reshape((step_total, group_size) + tensor.shape[1:])

    def one_group(running, inputs):
        group_lat, group_cot, group_live, group_cond = inputs
        group_out, stored = forward_pass(group_lat, group_cond, group_live, weights)
        mlp_grads, mlp_part = mlp_backward(group_cot, group_live, stored, weights)
        rest_grads, group_gin, group_gcond = attention_backward(group_cond, stored, weights, mlp_part)
        all_grads = mlp_grads + rest_grads
        running = tuple((old_sum + new_term for old_sum, new_term in zip(running, all_grads)))
        return (running, (group_out, group_gin, group_gcond))
    zero_grads = tuple((jnp.zeros(tensor.shape, jnp.float32) for tensor in (hidden_weight, output_weight, hidden_bias, output_bias, ada_weight, qkv_weight, proj_weight, ada_bias, query_bias, value_bias, proj_bias)))
    totals, stacked = lax.scan(one_group, zero_grads, (shaped(latents), shaped(cotangent), shaped(live_mask), shaped(conditioning)))
    g_hidden_w, g_output_w, g_hidden_b, g_output_b, g_ada_w, g_qkv_w, g_proj_w, g_ada_b, g_query_b, g_value_b, g_proj_b = totals
    block_output = stacked[0].reshape(latents.shape)
    grad_input = stacked[1].reshape(latents.shape)
    grad_cond = stacked[2].reshape(latent_count, D)
    return (block_output, grad_input, grad_cond, g_ada_w, g_ada_b, g_qkv_w, g_query_b, g_value_b, g_proj_w, g_proj_b, g_hidden_w, g_hidden_b, g_output_w, g_output_b)
```

```python
import functools
import math

import jax
import jax.numpy as jnp
from jax import lax
from jax.experimental import pallas as pl
from jax.experimental.pallas import tpu as pltpu
from jax.sharding import PartitionSpec as P

HEADS = 6
EPSILON = 1e-06
GELU_SCALE = math.sqrt(2.0 / math.pi)
GELU_CUBIC = 0.044715
LANES = 128
BF = jnp.bfloat16
F32 = jnp.float32
VMEM_LIMIT = 58 * 1024 * 1024


def dot(a, b):
    return jnp.dot(a, b, preferred_element_type=F32)


def dot_nt(a, b):
    return lax.dot_general(a, b, (((1,), (1,)), ((), ())), preferred_element_type=F32)


def dot_tn(a, b):
    return lax.dot_general(a, b, (((0,), (0,)), ((), ())), preferred_element_type=F32)


def row_mean(x):
    return jnp.mean(x, axis=-1, keepdims=True)


def layer_norm(x):
    centred = x - row_mean(x)
    inv = lax.rsqrt(row_mean(centred * centred) + EPSILON)
    return centred * inv, inv


def norm_backward(upstream, normed, inv):
    return inv * (upstream - row_mean(upstream) - normed * row_mean(upstream * normed))


def col_sum(x):
    return jnp.sum(x, axis=0, keepdims=True)


def load_pieces(idx_ref, pieces, whole, sems):
    rows = pieces[0].shape[0]
    copies = []
    for m, piece in enumerate(pieces):
        at = pl.multiple_of((idx_ref[1] ^ m) * rows, rows)
        copies.append(pltpu.make_async_copy(piece, whole.at[pl.ds(at, rows), :], sems.at[m]))
    return copies


def attn_fwd_kernel(n, idx, lat, mod, qb, vb, pb, *rest):
    qkv_p, proj_p = rest[:n], rest[n : 2 * n]
    attn_in_o, qkv_o, probs_o, mixed_o, attn_o, wqkv, wproj, sems = rest[2 * n :]

    @pl.when(pl.program_id(0) == 0)
    def _():
        copies = load_pieces(idx, qkv_p, wqkv, sems.at[0]) + load_pieces(
            idx, proj_p, wproj, sems.at[1]
        )
        for c in copies:
            c.start()
        for c in copies:
            c.wait()

    width = lat.shape[-1]
    head = width // HEADS
    pair = 2 * head
    shift1, scale1 = mod[0, 0:1, :], mod[0, 1:2, :]
    normed, _ = layer_norm(lat[0].astype(F32))
    attn_in = (normed * (1.0 + scale1) + shift1).astype(BF)
    attn_in_o[0] = attn_in
    q = (dot(attn_in, wqkv[:, :width]) + qb[...]).astype(BF)
    k = dot(attn_in, wqkv[:, width : 2 * width]).astype(BF)
    v = (dot(attn_in, wqkv[:, 2 * width :]) + vb[...]).astype(BF)
    qkv_o[0, :, :width] = q
    qkv_o[0, :, width : 2 * width] = k
    qkv_o[0, :, 2 * width :] = v
    lane = lax.broadcasted_iota(jnp.int32, (q.shape[0], pair), 1)
    factor = head ** (-0.5)
    mixed_pairs = []
    for j in range(HEADS // 2):
        cols = slice(j * pair, (j + 1) * pair)
        qp, kp, vp = q[:, cols] * BF(factor), k[:, cols], v[:, cols]
        outs = []
        for h in range(2):
            mask = (lane < head) if h == 0 else (lane >= head)
            s = dot_nt(jnp.where(mask, qp, BF(0)), kp)
            e = jnp.exp(s - jnp.max(s, axis=-1, keepdims=True))
            p = (e * (1.0 / jnp.sum(e, axis=-1, keepdims=True))).astype(BF)
            probs_o[0, 2 * j + h] = p
            outs.append(dot(p, vp))
        mixed_pairs.append(jnp.where(lane < head, outs[0], outs[1]).astype(BF))
    mixed = jnp.concatenate(mixed_pairs, axis=1)
    mixed_o[0] = mixed
    attn_o[0] = dot(mixed, wproj[...]) + pb[...]


def mlp_fwd_kernel(n, idx, lat, cot, attn, mod, hb, ob, *rest):
    hid_p, out_p = rest[:n], rest[n : 2 * n]
    (
        block_o, mlp_in_o, slope_o, small_o, obias_o, grad_o, whid, wout, acc, sems,
    ) = rest[2 * n :]
    step = pl.program_id(0)

    @pl.when(step == 0)
    def _():
        copies = load_pieces(idx, hid_p, whid, sems.at[0]) + load_pieces(
            idx, out_p, wout, sems.at[1]
        )
        for c in copies:
            c.start()
        for c in copies:
            c.wait()
        acc[...] = jnp.zeros_like(acc)
        obias_o[...] = jnp.zeros_like(obias_o)

    width = lat.shape[-1]
    live = jnp.where(step < idx[0], 1.0, 0.0).astype(F32)
    gate1, shift2, scale2, gate2 = (mod[0, i : i + 1, :] for i in range(2, 6))
    middle = lat[0].astype(F32) + gate1 * attn[0]
    normed, _ = layer_norm(middle)
    mlp_in = (normed * (1.0 + scale2) + shift2).astype(BF)
    mlp_in_o[0] = mlp_in
    grad_out = live * cot[0].astype(F32)
    d_mlp = grad_out * gate2
    d_mlp_b = d_mlp.astype(BF)
    obias_o[...] += col_sum(d_mlp)
    mlp_out = ob[...] + jnp.zeros_like(middle)
    for j in range(whid.shape[1] // width):
        cols = slice(j * width, (j + 1) * width)
        u = dot(mlp_in, whid[:, cols]) + hb[:, cols]
        u2 = u * u
        t = jnp.tanh(u * (GELU_SCALE + (GELU_SCALE * GELU_CUBIC) * u2))
        half = 0.5 * (1.0 + t)
        slope = half + (0.5 * u) * (1.0 - t * t) * (
            GELU_SCALE + (3.0 * GELU_SCALE * GELU_CUBIC) * u2
        )
        slope_o[0, :, cols] = slope.astype(BF)
        act = (u * half).astype(BF)
        mlp_out += dot(act, wout[cols, :])
        acc[cols, :] += dot_tn(act, d_mlp_b)
    block_o[0] = (live * (middle + gate2 * mlp_out)).astype(BF)
    small_o[0] = jnp.broadcast_to(col_sum(grad_out * mlp_out), small_o.shape[1:])

    @pl.when(step == pl.num_programs(0) - 1)
    def _():
        rows = acc.shape[0] // n
        for s in range(n):
            for j in range(width // LANES):
                grad_o[s, j * rows : (j + 1) * rows, :] = acc[
                    s * rows : (s + 1) * rows, j * LANES : (j + 1) * LANES
                ].astype(BF)


def mlp_bwd_kernel(n, idx, lat, cot, attn, mixed, mlp_in, slope, mod, *rest):
    hid_p, out_p, proj_p = rest[:n], rest[n : 2 * n], rest[2 * n : 3 * n]
    (
        dmid_o, dmix_o, small_o, hbias_o, pbias_o, grad_o, whid, wout, wproj, acc, accp, sems,
    ) = rest[3 * n :]
    step = pl.program_id(0)

    @pl.when(step == 0)
    def _():
        copies = (
            load_pieces(idx, hid_p, whid, sems.at[0])
            + load_pieces(idx, out_p, wout, sems.at[1])
            + load_pieces(idx, proj_p, wproj, sems.at[2])
        )
        for c in copies:
            c.start()
        for c in copies:
            c.wait()
        acc[...] = jnp.zeros_like(acc)
        accp[...] = jnp.zeros_like(accp)
        hbias_o[...] = jnp.zeros_like(hbias_o)
        pbias_o[...] = jnp.zeros_like(pbias_o)

    width = lat.shape[-1]
    live = jnp.where(step < idx[0], 1.0, 0.0).astype(F32)
    gate1, shift2, scale2, gate2 = (mod[0, i : i + 1, :] for i in range(2, 6))
    grad_out = live * cot[0].astype(F32)
    d_mlp_b = (grad_out * gate2).astype(BF)
    d_mlp_in = jnp.zeros_like(grad_out)
    mlp_in_v = mlp_in[0]
    for j in range(whid.shape[1] // width):
        cols = slice(j * width, (j + 1) * width)
        d_pre = dot_nt(d_mlp_b, wout[cols, :]) * slope[0, :, cols].astype(F32)
        hbias_o[:, cols] += col_sum(d_pre)
        d_pre_b = d_pre.astype(BF)
        acc[:, cols] += dot_tn(mlp_in_v, d_pre_b)
        d_mlp_in += dot_nt(d_pre_b, whid[:, cols])
    attn_v = attn[0]
    middle = lat[0].astype(F32) + gate1 * attn_v
    normed, inv = layer_norm(middle)
    d_shift2 = col_sum(d_mlp_in)
    d_scale2 = col_sum(d_mlp_in * normed)
    d_middle = grad_out + norm_backward(d_mlp_in * (1.0 + scale2), normed, inv)
    dmid_o[0] = d_middle
    d_gate1 = col_sum(d_middle * attn_v)
    d_attn = d_middle * gate1
    pbias_o[...] += col_sum(d_attn)
    d_attn_b = d_attn.astype(BF)
    accp[...] += dot_tn(mixed[0], d_attn_b)
    dmix_o[0] = dot_nt(d_attn_b, wproj[...]).astype(BF)
    small_o[0, 0:1] = d_gate1
    small_o[0, 1:2] = d_shift2
    small_o[0, 2:3] = d_scale2
    small_o[0, 3:8] = jnp.zeros((5, width), F32)

    @pl.when(step == pl.num_programs(0) - 1)
    def _():
        rows = acc.shape[0] // n
        blocks = acc.shape[1] // LANES
        for s in range(n):
            here = slice(s * rows, (s + 1) * rows)
            for j in range(blocks):
                grad_o[s, j * rows : (j + 1) * rows, :] = acc[
                    here, j * LANES : (j + 1) * LANES
                ].astype(BF)
            for j in range(width // LANES):
                at = (blocks + j) * rows
                grad_o[s, at : at + rows, :] = accp[here, j * LANES : (j + 1) * LANES].astype(BF)
            at = (blocks + width // LANES) * rows
            if at < grad_o.shape[1]:
                grad_o[s, at:, :] = jnp.zeros((grad_o.shape[1] - at, LANES), BF)


def attn_bwd_kernel(n, idx, lat, dmid, dmix, attn_in, qkv, probs, mod, *rest):
    qkv_p = rest[:n]
    gin_o, small_o, qbias_o, vbias_o, grad_o, wqkv, acc, dproj, sems = rest[n:]
    step = pl.program_id(0)

    @pl.when(step == 0)
    def _():
        copies = load_pieces(idx, qkv_p, wqkv, sems.at[0])
        for c in copies:
            c.start()
        for c in copies:
            c.wait()
        acc[...] = jnp.zeros_like(acc)
        qbias_o[...] = jnp.zeros_like(qbias_o)
        vbias_o[...] = jnp.zeros_like(vbias_o)

    width = lat.shape[-1]
    head = width // HEADS
    pair = 2 * head
    factor = head ** (-0.5)
    lane = lax.broadcasted_iota(jnp.int32, (lat.shape[1], pair), 1)
    low = lane < head
    for j in range(HEADS // 2):
        at = j * pair
        q = qkv[0, :, at : at + pair]
        k = qkv[0, :, width + at : width + at + pair]
        v = qkv[0, :, 2 * width + at : 2 * width + at + pair]
        dm = dmix[0, :, at : at + pair]
        parts = []
        for h in range(2):
            mask = low if h == 0 else ~low
            p_b = probs[0, 2 * j + h]
            p = p_b.astype(F32)
            dp = dot_nt(jnp.where(mask, dm, BF(0)), v)
            row_dot = jnp.sum(p * dp, axis=-1, keepdims=True)
            ds = (p * (dp - row_dot) * factor).astype(BF)
            parts.append((dot(ds, k), dot_tn(ds, q), dot_tn(p_b, dm)))
        dq, dk, dv = (jnp.where(low, a, b) for a, b in zip(*parts))
        qbias_o[:, at : at + pair] += col_sum(dq)
        vbias_o[:, at : at + pair] += col_sum(dv)
        dproj[:, at : at + pair] = dq.astype(BF)
        dproj[:, width + at : width + at + pair] = dk.astype(BF)
        dproj[:, 2 * width + at : 2 * width + at + pair] = dv.astype(BF)
    d_proj = dproj[...]
    d_attn_in = dot_nt(d_proj, wqkv[...])
    acc[...] += dot_tn(attn_in[0], d_proj)
    scale1 = mod[0, 1:2, :]
    normed, inv = layer_norm(lat[0].astype(F32))
    small_o[0, 0:1] = col_sum(d_attn_in)
    small_o[0, 1:2] = col_sum(d_attn_in * normed)
    small_o[0, 2:8] = jnp.zeros((6, width), F32)
    gin_o[0] = dmid[0] + norm_backward(d_attn_in * (1.0 + scale1), normed, inv)

    @pl.when(step == pl.num_programs(0) - 1)
    def _():
        rows = acc.shape[0] // n
        blocks = acc.shape[1] // LANES
        for s in range(n):
            for j in range(blocks):
                grad_o[s, j * rows : (j + 1) * rows, :] = acc[
                    s * rows : (s + 1) * rows, j * LANES : (j + 1) * LANES
                ].astype(BF)
            at = blocks * rows
            if at < grad_o.shape[1]:
                grad_o[s, at:, :] = jnp.zeros((grad_o.shape[1] - at, LANES), BF)


def per_latent(shape):
    rest = tuple(shape[1:])
    zeros = (0,) * len(rest)
    return pl.BlockSpec((1,) + rest, lambda i, idx: (i,) + zeros)


def resident(shape):
    zeros = (0,) * len(shape)
    return pl.BlockSpec(tuple(shape), lambda i, idx: zeros)


def run(kernel, name, steps, idx, blocked, whole, pieces, outs_blocked, outs_whole, scratch, flops):
    out_shape = [jax.ShapeDtypeStruct(s, d) for s, d in outs_blocked + outs_whole]
    moved = sum(a.size * a.dtype.itemsize for a in list(blocked) + list(whole) + list(pieces))
    moved += sum(math.prod(s.shape) * s.dtype.itemsize for s in out_shape)
    return pl.pallas_call(
        kernel,
        name=name,
        out_shape=out_shape,
        grid_spec=pltpu.PrefetchScalarGridSpec(
            num_scalar_prefetch=1,
            grid=(steps,),
            in_specs=[per_latent(a.shape) for a in blocked]
            + [resident(a.shape) for a in whole]
            + [pl.BlockSpec(memory_space=pl.ANY) for _ in pieces],
            out_specs=[per_latent(s) for s, _ in outs_blocked]
            + [resident(s) for s, _ in outs_whole],
            scratch_shapes=scratch,
        ),
        compiler_params=pltpu.CompilerParams(
            dimension_semantics=("arbitrary",), vmem_limit_bytes=VMEM_LIMIT
        ),
        cost_estimate=pl.CostEstimate(flops=flops, transcendentals=0, bytes_accessed=moved),
    )(idx, *blocked, *whole, *pieces)


def time_embed(step_ids, model_width):
    half_width = model_width // 2
    frequency = jnp.exp(-math.log(10000.0) * jnp.arange(half_width, dtype=F32) / half_width)
    angles = step_ids.astype(F32)[:, None] * frequency[None, :]
    return jnp.concatenate([jnp.cos(angles), jnp.sin(angles)], axis=1)


def swap(x, axis, mask, size):
    return lax.ppermute(x, axis, [(i, i ^ mask) for i in range(size)])


def gather_xor(own, axis, size):
    pieces = [own]
    for m in range(1, size):
        low = m & -m
        pieces.append(swap(pieces[m ^ low], axis, low, size))
    return pieces


def reduce_scatter(x, axis, size, index):
    bit = 1
    while bit < size:
        x = x.reshape((x.shape[0] // 2, 2) + x.shape[1:])
        mine = (index // bit) % 2
        keep = lax.dynamic_index_in_dim(x, mine, 1, keepdims=False)
        send = lax.dynamic_index_in_dim(x, 1 - mine, 1, keepdims=False)
        got = swap(send, axis, bit, size)
        x = (keep.astype(F32) + got.astype(F32)).astype(BF)
        bit *= 2
    return x[0]


def all_reduce(x, axis, size, index):
    bit = 1
    bits = []
    while bit < size:
        x = x.reshape((2, x.shape[0] // 2) + x.shape[1:])
        mine = (index // bit) % 2
        keep = lax.dynamic_index_in_dim(x, mine, 0, keepdims=False)
        send = lax.dynamic_index_in_dim(x, 1 - mine, 0, keepdims=False)
        got = swap(send, axis, bit, size)
        x = (keep.astype(F32) + got.astype(F32)).astype(BF)
        bits.append((bit, mine))
        bit *= 2
    for bit, mine in reversed(bits):
        got = swap(x, axis, bit, size)
        first = jnp.where(mine == 0, x, got)
        second = jnp.where(mine == 0, got, x)
        x = jnp.concatenate([first, second], axis=0)
    return x


def unblock(x, rows):
    blocks = x.shape[0] // rows
    return x.reshape(blocks, rows, LANES).transpose(1, 0, 2).reshape(rows, blocks * LANES)


def place(pieces, index, size):
    stacked = jnp.stack(pieces)
    return jnp.concatenate(
        [lax.dynamic_index_in_dim(stacked, index ^ j, 0, keepdims=False) for j in range(size)]
    )


def round_up(value, step):
    return -(-value // step) * step


def per_device(
    n_shard,
    n_rep,
    latents,
    cotangent,
    counts,
    labels,
    timesteps,
    class_table,
    ada_weight,
    ada_bias,
    qkv_weight,
    query_bias,
    value_bias,
    proj_weight,
    proj_bias,
    hidden_weight,
    hidden_bias,
    output_weight,
    output_bias,
):
    n = n_shard
    slots, seq, width = latents.shape
    hidden = hidden_weight.shape[1]
    part = width // n
    shard = lax.axis_index("shard").astype(jnp.int32)
    rep = lax.axis_index("rep").astype(jnp.int32)
    idx = jnp.stack([counts[0], shard])

    qkv_p = gather_xor(qkv_weight, "shard", n)
    proj_p = gather_xor(proj_weight, "shard", n)
    hid_p = gather_xor(hidden_weight, "shard", n)
    out_p = gather_xor(output_weight, "shard", n)

    one_hot = (labels[:, None] == jnp.arange(class_table.shape[0], dtype=jnp.int32)[None, :])
    cond = dot(one_hot.astype(BF), class_table) + time_embed(timesteps, width)
    sig = jax.nn.sigmoid(cond)
    silu = (cond * sig).astype(BF)
    silu_parts = silu.reshape(slots, n, part)
    biases = jnp.concatenate(
        [ada_bias, hidden_bias, query_bias, value_bias, proj_bias, output_bias]
    )
    group_silu, group_bias = [], []
    for m in range(n):
        piece = lax.dynamic_index_in_dim(silu_parts, shard ^ m, 1, keepdims=False)
        message = jnp.concatenate([piece.reshape(-1), biases])
        if m:
            message = swap(message, "shard", m, n)
        group_silu.append(message[: slots * part].reshape(slots, part))
        group_bias.append(message[slots * part :])
    group_silu = jnp.concatenate(group_silu, axis=0)
    partial = dot(group_silu, ada_weight).reshape(n, slots, -1)
    modulation = partial[0]
    for m in range(1, n):
        modulation = modulation + swap(partial[m], "shard", m, n)
    sizes = [ada_bias.shape[0], hidden_bias.shape[0]] + [part] * 4
    full_bias = []
    at = 0
    for size in sizes:
        full_bias.append(place([b[at : at + size] for b in group_bias], shard, n).astype(F32))
        at += size
    ada_b, hid_b, q_b, v_b, p_b, o_b = full_bias
    modulation = modulation + ada_b
    mod = jnp.pad(modulation.reshape(slots, 6, width), ((0, 0), (0, 2), (0, 0)))

    all_silu = group_silu
    bit = 1
    while bit < n_rep:
        all_silu = jnp.concatenate([all_silu, swap(all_silu, "rep", bit, n_rep)], axis=0)
        bit *= 2

    rows = slots * seq
    tok = (slots, seq, width)
    small = (slots, 8, width)
    dma = pltpu.SemaphoreType.DMA
    attn_in, qkv, probs, mixed, attn = run(
        functools.partial(attn_fwd_kernel, n), "attn_fwd", slots, idx,
        (latents, mod), (q_b[None], v_b[None], p_b[None]), (*qkv_p, *proj_p),
        [(tok, BF), ((slots, seq, 3 * width), BF), ((slots, HEADS, seq, seq), BF), (tok, BF),
         (tok, F32)],
        [],
        [pltpu.VMEM((width, 3 * width), BF), pltpu.VMEM((width, width), BF), dma((2, n))],
        2 * rows * width * 4 * width + 4 * rows * seq * width,
    )
    packed_out = output_weight.shape[0] * (width // LANES)
    block_output, mlp_in, slope, small2, obias, grad_out_w = run(
        functools.partial(mlp_fwd_kernel, n), "mlp_fwd", slots, idx,
        (latents, cotangent, attn, mod), (hid_b[None], o_b[None]), (*hid_p, *out_p),
        [(tok, BF), (tok, BF), ((slots, seq, hidden), BF), (small, F32)],
        [((1, width), F32), ((n, packed_out, LANES), BF)],
        [pltpu.VMEM((width, hidden), BF), pltpu.VMEM((hidden, width), BF),
         pltpu.VMEM((hidden, width), F32), dma((2, n))],
        6 * rows * width * hidden,
    )
    out_share = reduce_scatter(grad_out_w, "shard", n, shard)
    out_total = all_reduce(out_share, "rep", n_rep, rep)

    align = 8 * n_rep
    packed_hid = round_up(part * (hidden + width) // LANES, align)
    d_middle, d_mixed, small3, hbias, pbias, grad_hid = run(
        functools.partial(mlp_bwd_kernel, n), "mlp_bwd", slots, idx,
        (latents, cotangent, attn, mixed, mlp_in, slope, mod), (), (*hid_p, *out_p, *proj_p),
        [(tok, F32), (tok, BF), (small, F32)],
        [((1, hidden), F32), ((1, width), F32), ((n, packed_hid, LANES), BF)],
        [pltpu.VMEM((width, hidden), BF), pltpu.VMEM((hidden, width), BF),
         pltpu.VMEM((width, width), BF), pltpu.VMEM((width, hidden), F32),
         pltpu.VMEM((width, width), F32), dma((3, n))],
        6 * rows * width * hidden + 4 * rows * width * width,
    )
    hid_share = reduce_scatter(grad_hid, "shard", n, shard)
    hid_total = all_reduce(hid_share, "rep", n_rep, rep)

    packed_qkv = round_up(part * 3 * width // LANES, align)
    grad_input, small4, qbias, vbias, grad_qkv = run(
        functools.partial(attn_bwd_kernel, n), "attn_bwd", slots, idx,
        (latents, d_middle, d_mixed, attn_in, qkv, probs, mod), (), tuple(qkv_p),
        [(tok, F32), (small, F32)],
        [((1, width), F32), ((1, width), F32), ((n, packed_qkv, LANES), BF)],
        [pltpu.VMEM((width, 3 * width), BF), pltpu.VMEM((width, 3 * width), F32),
         pltpu.VMEM((seq, 3 * width), BF), dma((1, n))],
        12 * rows * width * width + 8 * rows * seq * width,
    )
    qkv_share = reduce_scatter(grad_qkv, "shard", n, shard)
    qkv_total = all_reduce(qkv_share, "rep", n_rep, rep)

    d_mod = jnp.concatenate(
        [small4[:, 0], small4[:, 1], small3[:, 0], small3[:, 1], small3[:, 2], small2[:, 0]],
        axis=1,
    )
    bias_sums = jnp.concatenate([hbias[0], qbias[0], vbias[0], pbias[0], obias[0]])
    message = jnp.concatenate([d_mod.reshape(-1), bias_sums]).astype(BF)[None]
    bit = 1
    while bit < n:
        message = jnp.concatenate([message, swap(message, "shard", bit, n)], axis=0)
        bit *= 2
    d_mod_size = slots * 6 * width
    group_d_mod = message[:, :d_mod_size].reshape(n * slots, 6 * width)
    partial_cond = lax.dot_general(
        group_d_mod, ada_weight, (((1,), (1,)), ((), ())), preferred_element_type=F32
    ).reshape(n, slots, part)
    cond_pieces = [partial_cond[0]]
    for m in range(1, n):
        cond_pieces.append(swap(partial_cond[m], "shard", m, n))
    cond_stack = jnp.stack(cond_pieces)
    d_silu = jnp.concatenate(
        [lax.dynamic_index_in_dim(cond_stack, shard ^ j, 0, keepdims=False) for j in range(n)],
        axis=1,
    )
    grad_cond = d_silu * sig * (1.0 + cond * (1.0 - sig))
    bit = 1
    while bit < n_rep:
        message = jnp.concatenate([message, swap(message, "rep", bit, n_rep)], axis=0)
        bit *= 2
    all_d_mod = message[:, :d_mod_size].reshape(-1, 6 * width)
    grad_ada = lax.dot_general(
        all_silu, all_d_mod, (((0,), (0,)), ((), ())), preferred_element_type=F32
    )
    grad_ada_b = jnp.sum(all_d_mod.astype(F32), axis=0)
    bias_total = jnp.sum(message[:, d_mod_size:].astype(F32), axis=0)

    def own(vector):
        return lax.dynamic_index_in_dim(vector.reshape(n, -1), shard, 0, keepdims=False)

    hid_rows = part * hidden // LANES
    b_hid = bias_total[:hidden]
    b_q, b_v, b_p, b_o = (
        bias_total[hidden + i * width : hidden + (i + 1) * width] for i in range(4)
    )
    return (
        block_output,
        grad_input,
        grad_cond,
        grad_ada,
        own(grad_ada_b),
        unblock(qkv_total[: part * 3 * width // LANES], part).astype(F32),
        own(b_q),
        own(b_v),
        unblock(hid_total[hid_rows : hid_rows + part * width // LANES], part).astype(F32),
        own(b_p),
        unblock(hid_total[:hid_rows], part).astype(F32),
        own(b_hid),
        unblock(out_total, output_weight.shape[0]).astype(F32),
        own(b_o),
    )


def solution(mesh):
    both = ("rep", "shard")
    in_specs = (
        P(both, None, None),
        P(both, None, None),
        P(both),
        P(both),
        P(both),
        P(),
        P("shard", None),
        P("shard"),
        P("shard", None),
        P("shard"),
        P("shard"),
        P("shard", None),
        P("shard"),
        P("shard", None),
        P("shard"),
        P("shard", None),
        P("shard"),
    )
    out_specs = (
        P(both, None, None),
        P(both, None, None),
        P(both, None),
        P("shard", None),
        P("shard"),
        P("shard", None),
        P("shard"),
        P("shard"),
        P("shard", None),
        P("shard"),
        P("shard", None),
        P("shard"),
        P("shard", None),
        P("shard"),
    )
    body = functools.partial(per_device, mesh.shape["shard"], mesh.shape["rep"])
    return jax.shard_map(
        body, mesh=mesh, in_specs=in_specs, out_specs=out_specs, check_vma=False
    )
```

```python
import functools
import math

import jax
import jax.numpy as jnp
from jax import lax
from jax.experimental import pallas as pl
from jax.experimental.pallas import tpu as pltpu
from jax.sharding import PartitionSpec as P


HEADS = 6
EPSILON = 1e-06
GELU_SCALE = math.sqrt(2.0 / math.pi)
GELU_CUBIC = 0.044715
LANES = 128
LATENTS_PER_STEP = 2
CHUNK = 512
RIDER_ROWS = 24
BF = jnp.bfloat16
F32 = jnp.float32
VMEM_LIMIT = 58 * 1024 * 1024


def dot(a, b):
    return jnp.dot(a, b, preferred_element_type=F32)


def dot_nt(a, b):
    return lax.dot_general(a, b, (((1,), (1,)), ((), ())), preferred_element_type=F32)


def dot_tn(a, b):
    return lax.dot_general(a, b, (((0,), (0,)), ((), ())), preferred_element_type=F32)


def row_mean(x):
    return jnp.mean(x, axis=-1, keepdims=True)


def layer_norm(x):
    centred = x - row_mean(x)
    inv = lax.rsqrt(row_mean(centred * centred) + EPSILON)
    return centred * inv, inv


def norm_backward(upstream, normed, inv):
    return inv * (upstream - row_mean(upstream) - normed * row_mean(upstream * normed))


def col_sum(x):
    return jnp.sum(x, axis=0, keepdims=True)


def load_pieces(idx_ref, pieces, whole, sems, first=0):
    rows = whole.shape[0] // len(pieces)
    copies = []
    for m, piece in enumerate(pieces):
        at = pl.multiple_of((idx_ref[1] ^ m) * rows, rows)
        source = piece.at[first : first + rows, :]
        copies.append(pltpu.make_async_copy(source, whole.at[pl.ds(at, rows), :], sems.at[m]))
    return copies


def store_blocks(ref, at, first, value):
    rows = value.shape[0]
    for j in range(value.shape[1] // LANES):
        ref[at, first : first + rows, :] = value[:, j * LANES : (j + 1) * LANES].astype(BF)
        first += rows
    return first


def store_rows(ref, first, value):
    for j in range(value.shape[1] // LANES):
        ref[first : first + 1, :] = value[:, j * LANES : (j + 1) * LANES]
        first += 1
    return first


def store_shares(idx_ref, n, keep, send, *totals, tail=None):
    for m in range(n):
        ref, at = (keep, send)[m % 2], m // 2
        first = 0
        for total in totals:
            rows = total.shape[0] // n
            start = pl.multiple_of((idx_ref[1] ^ m) * rows, rows)
            first = store_blocks(ref, at, first, total[pl.ds(start, rows), :])
        if tail is not None:
            ref[at, first : first + tail.shape[0], :] = tail[...].astype(BF)
            first += tail.shape[0]
        if first < ref.shape[1]:
            ref[at, first:, :] = jnp.zeros((ref.shape[1] - first, LANES), BF)


def attn_fwd_kernel(n, idx, lat, mod, qvpo, *rest):
    qkv_p = rest[:n]
    attn_in_o, qkv_o, probs_o, mixed_o, wqkv, sems = rest[n:]

    @pl.when(pl.program_id(0) == 0)
    def _():
        copies = load_pieces(idx, qkv_p, wqkv, sems.at[0])
        for c in copies:
            c.start()
        for c in copies:
            c.wait()

    group, seq, width = lat.shape
    rows = group * seq
    head = width // HEADS
    pair = 2 * head
    normed, _ = layer_norm(lat[...].astype(F32))
    attn_in = (normed * (1.0 + mod[:, 1:2, :]) + mod[:, 0:1, :]).astype(BF)
    attn_in_o[...] = attn_in
    attn_in = attn_in.reshape(rows, width)
    proj_all = dot(attn_in, wqkv[...])
    q = (proj_all[:, :width] + qvpo[0:1, :]).astype(BF)
    k = proj_all[:, width : 2 * width].astype(BF)
    v = (proj_all[:, 2 * width :] + qvpo[1:2, :]).astype(BF)
    qkv_o[:, :, :width] = q.reshape(group, seq, width)
    qkv_o[:, :, width : 2 * width] = k.reshape(group, seq, width)
    qkv_o[:, :, 2 * width :] = v.reshape(group, seq, width)
    low = lax.broadcasted_iota(jnp.int32, (seq, pair), 1) < head
    factor = head ** (-0.5)
    for g in range(group):
        here = slice(g * seq, (g + 1) * seq)
        for j in range(HEADS // 2):
            cols = slice(j * pair, (j + 1) * pair)
            qp, kp, vp = q[here, cols] * BF(factor), k[here, cols], v[here, cols]
            outs = []
            for h in range(2):
                mask = low if h == 0 else ~low
                s = dot_nt(kp, jnp.where(mask, qp, BF(0)))
                e = jnp.exp(s - jnp.max(s, axis=0, keepdims=True))
                p = (e * (1.0 / jnp.sum(e, axis=0, keepdims=True))).astype(BF)
                probs_o[g, 2 * j + h] = p
                outs.append(dot_tn(p, vp))
            mixed_o[g, :, cols] = jnp.where(low, outs[0], outs[1]).astype(BF)


def mlp_kernel(n, idx, lat, cot, mixed, mod, qvpo, hb, *rest):
    hid_p, out_p = rest[:n], rest[n : 2 * n]
    (
        block_o, dmid_o, dmix_o, small_o, obias_o, hbias_o, pbias_o, keep_o, send_o,
        whid, wout, wproj, acco, acch, accp, sems,
    ) = rest[2 * n :]
    step = pl.program_id(0)

    @pl.when(step == 0)
    def _():
        copies = (
            load_pieces(idx, hid_p, whid, sems.at[0])
            + load_pieces(idx, out_p, wout, sems.at[1])
            + load_pieces(idx, out_p, wproj, sems.at[2], first=wout.shape[0] // n)
        )
        for c in copies:
            c.start()
        for ref in (acco, acch, accp, obias_o, hbias_o, pbias_o):
            ref[...] = jnp.zeros_like(ref)
        for c in copies:
            c.wait()

    group, seq, width = lat.shape
    rows = group * seq

    def flat(x):
        return x.reshape(rows, width)

    def deep(x):
        return x.reshape(group, seq, width)

    slot = lax.broadcasted_iota(jnp.int32, (group, 1, 1), 0) + step * group
    live = jnp.where(slot < idx[0], 1.0, 0.0).astype(F32)
    gate1, shift2, scale2, gate2 = (mod[:, i : i + 1, :] for i in range(2, 6))
    mixed_v = flat(mixed[...])
    attn = deep(dot(mixed_v, wproj[...]) + qvpo[2:3, :])
    middle = lat[...].astype(F32) + gate1 * attn
    normed, inv = layer_norm(middle)
    mlp_in = flat((normed * (1.0 + scale2) + shift2).astype(BF))
    grad_out = live * cot[...].astype(F32)
    d_mlp = flat(grad_out * gate2)
    d_mlp_b = d_mlp.astype(BF)
    obias_o[...] += col_sum(d_mlp)
    mlp_out = qvpo[3:4, :] + jnp.zeros((rows, width), F32)
    d_mlp_in = jnp.zeros((rows, width), F32)
    hidden = whid.shape[1]
    chunk = CHUNK if hidden % CHUNK == 0 else width
    bias = jnp.concatenate([hb[j : j + 1, :] for j in range(hidden // width)], axis=1)
    for j in range(hidden // chunk):
        cols = slice(j * chunk, (j + 1) * chunk)
        u = dot(mlp_in, whid[:, cols]) + bias[:, cols]
        u2 = u * u
        t = jnp.tanh(u * (GELU_SCALE + (GELU_SCALE * GELU_CUBIC) * u2))
        half = 0.5 * (1.0 + t)
        slope = half + (0.5 * u) * (1.0 - t * t) * (
            GELU_SCALE + (3.0 * GELU_SCALE * GELU_CUBIC) * u2
        )
        act = (u * half).astype(BF)
        mlp_out += dot(act, wout[cols, :])
        acco[cols, :] += dot_tn(act, d_mlp_b)
        d_pre = dot_nt(d_mlp_b, wout[cols, :]) * slope
        hbias_o[:, cols] += col_sum(d_pre)
        d_pre_b = d_pre.astype(BF)
        acch[:, cols] += dot_tn(mlp_in, d_pre_b)
        d_mlp_in += dot_nt(d_pre_b, whid[:, cols])
    mlp_out = deep(mlp_out)
    d_mlp_in = deep(d_mlp_in)
    block_o[...] = (live * (middle + gate2 * mlp_out)).astype(BF)
    d_middle = grad_out + norm_backward(d_mlp_in * (1.0 + scale2), normed, inv)
    dmid_o[...] = d_middle
    d_attn = flat(d_middle * gate1)
    pbias_o[...] += col_sum(d_attn)
    d_attn_b = d_attn.astype(BF)
    accp[...] += dot_tn(mixed_v, d_attn_b)
    dmix_o[...] = deep(dot_nt(d_attn_b, wproj[...]).astype(BF))
    for g in range(group):
        small_o[g, 0:1] = col_sum(d_middle[g] * attn[g])
        small_o[g, 1:2] = col_sum(d_mlp_in[g])
        small_o[g, 2:3] = col_sum(d_mlp_in[g] * normed[g])
        small_o[g, 3:4] = col_sum(grad_out[g] * mlp_out[g])
        small_o[g, 4:8] = jnp.zeros((4, width), F32)

    @pl.when(step == pl.num_programs(0) - 1)
    def _():
        store_shares(idx, n, keep_o, send_o, acco, acch, accp)


def attn_bwd_kernel(
    n, idx, lat, dmid, dmix, attn_in, qkv, probs, mod, small, silu, obias, hbias, pbias, *rest
):
    qkv_p = rest[:n]
    (
        gin_o, riders_o, keep_o, send_o, wqkv, acc, dproj, qbias, vbias, lines, sums, sems,
    ) = rest[n:]
    step = pl.program_id(0)

    @pl.when(step == 0)
    def _():
        copies = load_pieces(idx, qkv_p, wqkv, sems.at[0])
        for c in copies:
            c.start()
        for c in copies:
            c.wait()
        acc[...] = jnp.zeros_like(acc)
        qbias[...] = jnp.zeros_like(qbias)
        vbias[...] = jnp.zeros_like(vbias)

    group, seq, width = lat.shape
    rows = group * seq
    head = width // HEADS
    pair = 2 * head
    factor = head ** (-0.5)
    low = lax.broadcasted_iota(jnp.int32, (seq, pair), 1) < head
    for g in range(group):
        here = slice(g * seq, (g + 1) * seq)
        for j in range(HEADS // 2):
            at = j * pair
            q = qkv[g, :, at : at + pair]
            k = qkv[g, :, width + at : width + at + pair]
            v = qkv[g, :, 2 * width + at : 2 * width + at + pair]
            dm = dmix[g, :, at : at + pair]
            parts = []
            for h in range(2):
                mask = low if h == 0 else ~low
                p_b = probs[g, 2 * j + h]
                p = p_b.astype(F32)
                dp = dot_nt(v, jnp.where(mask, dm, BF(0)))
                row_dot = jnp.sum(p * dp, axis=0, keepdims=True)
                ds = (p * (dp - row_dot) * factor).astype(BF)
                parts.append((dot_tn(ds, k), dot(ds, q), dot(p_b, dm)))
            dq, dk, dv = (jnp.where(low, a, b) for a, b in zip(*parts))
            qbias[:, at : at + pair] += col_sum(dq)
            vbias[:, at : at + pair] += col_sum(dv)
            dproj[here, at : at + pair] = dq.astype(BF)
            dproj[here, width + at : width + at + pair] = dk.astype(BF)
            dproj[here, 2 * width + at : 2 * width + at + pair] = dv.astype(BF)
    d_proj = dproj[...]
    d_attn_in = dot_nt(d_proj, wqkv[...]).reshape(group, seq, width)
    acc[...] += dot_tn(attn_in[...].reshape(rows, width), d_proj)
    normed, inv = layer_norm(lat[...].astype(F32))
    gin_o[...] = dmid[...] + norm_backward(d_attn_in * (1.0 + mod[:, 1:2, :]), normed, inv)
    for g in range(group):
        at = store_rows(lines, 0, col_sum(d_attn_in[g]))
        at = store_rows(lines, at, col_sum(d_attn_in[g] * normed[g]))
        for i in range(4):
            at = store_rows(lines, at, small[g, i : i + 1, :])
        at = store_rows(lines, at, silu[pl.ds(step * group + g, 1), :])
        lines[at:, :] = jnp.zeros((RIDER_ROWS - at, LANES), F32)
        riders_o[g * RIDER_ROWS : (g + 1) * RIDER_ROWS, :] = lines[...].astype(BF)

    @pl.when(step == pl.num_programs(0) - 1)
    def _():
        at = 0
        for value in (hbias, qbias, vbias, pbias, obias):
            at = store_rows(sums, at, value[...])
        store_shares(idx, n, keep_o, send_o, acc, tail=sums)


def per_step(shape, steps):
    rest = tuple(shape[1:])
    zeros = (0,) * len(rest)
    return pl.BlockSpec((shape[0] // steps,) + rest, lambda i, idx: (i,) + zeros)


def resident(shape):
    zeros = (0,) * len(shape)
    return pl.BlockSpec(tuple(shape), lambda i, idx: zeros)


def run(kernel, steps, idx, blocked, whole, pieces, outs_blocked, outs_whole, scratch, flops):
    out_shape = [jax.ShapeDtypeStruct(s, d) for s, d in outs_blocked + outs_whole]
    moved = sum(a.size * a.dtype.itemsize for a in list(blocked) + list(whole) + list(pieces))
    moved += sum(math.prod(s.shape) * s.dtype.itemsize for s in out_shape)
    return pl.pallas_call(
        kernel,
        out_shape=out_shape,
        grid_spec=pltpu.PrefetchScalarGridSpec(
            num_scalar_prefetch=1,
            grid=(steps,),
            in_specs=[per_step(a.shape, steps) for a in blocked]
            + [resident(a.shape) for a in whole]
            + [pl.BlockSpec(memory_space=pl.ANY) for _ in pieces],
            out_specs=[per_step(s, steps) for s, _ in outs_blocked]
            + [resident(s) for s, _ in outs_whole],
            scratch_shapes=scratch,
        ),
        compiler_params=pltpu.CompilerParams(
            dimension_semantics=("arbitrary",), vmem_limit_bytes=VMEM_LIMIT
        ),
        cost_estimate=pl.CostEstimate(flops=flops, transcendentals=0, bytes_accessed=moved),
    )(idx, *blocked, *whole, *pieces)


def finish_kernel(n, biases, side, x, got, *rest):
    outs, full = rest[:-1], rest[-1]
    half = x.shape[0]
    full[pl.ds(pl.multiple_of(side[0] * half, half), half), :] = x[...]
    full[pl.ds(pl.multiple_of((1 - side[0]) * half, half), half), :] = got[...]
    first = 0
    for out in outs if biases is None else outs[:1]:
        rows = out.shape[0]
        for j in range(out.shape[1] // LANES):
            out[:, j * LANES : (j + 1) * LANES] = full[first : first + rows, :].astype(F32)
            first += rows
    if biases is None:
        return
    hidden, width = biases
    lines = full[first : first + (hidden + 4 * width) // LANES, :].astype(F32)
    share = hidden // n // LANES
    for i in range(share):
        line = jnp.zeros((1, LANES), F32)
        for j in range(n):
            at = j * share + i
            line = jnp.where(side[1] == j, lines[at : at + 1, :], line)
        outs[1][:, i * LANES : (i + 1) * LANES] = line
    part = width // n
    row = lax.broadcasted_iota(jnp.int32, (width, part), 0)
    col = lax.broadcasted_iota(jnp.int32, (width, part), 1)
    pick = jnp.where(row == col + side[1] * part, 1.0, 0.0).astype(BF)
    at = hidden // LANES
    for out in outs[2:]:
        vector = jnp.concatenate(
            [lines[at + i : at + i + 1, :] for i in range(width // LANES)], axis=1
        )
        wide = jnp.broadcast_to(vector, (8, width)).astype(BF)
        out[...] = dot(wide, pick)[0:1, :]
        at += width // LANES


def finish(side, x, got, shapes, biases, n):
    shapes = list(shapes)
    if biases is not None:
        shapes += [(1, biases[0] // n)] + [(1, biases[1] // n)] * 4
    spec = pl.BlockSpec(memory_space=pltpu.VMEM)
    return pl.pallas_call(
        functools.partial(finish_kernel, n, biases),
        out_shape=[jax.ShapeDtypeStruct(shape, F32) for shape in shapes],
        in_specs=[pl.BlockSpec(memory_space=pltpu.SMEM), spec, spec],
        out_specs=[spec] * len(shapes),
        scratch_shapes=[pltpu.VMEM((2 * x.shape[0], LANES), BF)],
        cost_estimate=pl.CostEstimate(
            flops=0, transcendentals=0, bytes_accessed=12 * x.size
        ),
    )(side, x, got)


def time_embed(step_ids, model_width):
    half_width = model_width // 2
    frequency = jnp.exp(-math.log(10000.0) * jnp.arange(half_width, dtype=F32) / half_width)
    angles = step_ids.astype(F32)[:, None] * frequency[None, :]
    return jnp.concatenate([jnp.cos(angles), jnp.sin(angles)], axis=1)


def swap(x, axis, mask, size):
    return lax.ppermute(x, axis, [(i, i ^ mask) for i in range(size)])


def first_hop(own, axis, size):
    return swap(own, axis, size // 2, size)


def gather_xor(own, got, axis, size):
    bit = size // 2
    pieces = {0: own, bit: got}
    bit //= 2
    while bit:
        for m in list(pieces):
            pieces[m ^ bit] = swap(pieces[m], axis, bit, size)
        bit //= 2
    return [pieces[m] for m in range(size)]


def bit_of(index, bit):
    return (index // bit) % 2


def joined(mine, x, got):
    first = jnp.where(mine == 0, x, got)
    second = jnp.where(mine == 0, got, x)
    return jnp.concatenate([first, second], axis=0)


def halves(x, mine):
    x = x.reshape((2, x.shape[0] // 2) + x.shape[1:])
    keep = lax.dynamic_index_in_dim(x, mine, 0, keepdims=False)
    send = lax.dynamic_index_in_dim(x, 1 - mine, 0, keepdims=False)
    return keep, send


def plus(a, b):
    return (a.astype(F32) + b.astype(F32)).astype(BF)


def round_up(value, step):
    return -(-value // step) * step


def per_device(
    n_shard,
    n_rep,
    latents,
    cotangent,
    counts,
    labels,
    timesteps,
    class_table,
    ada_weight,
    ada_bias,
    qkv_weight,
    query_bias,
    value_bias,
    proj_weight,
    proj_bias,
    hidden_weight,
    hidden_bias,
    output_weight,
    output_bias,
):
    n = n_shard
    slots, seq, width = latents.shape
    hidden = hidden_weight.shape[1]
    part = width // n
    shard = lax.axis_index("shard").astype(jnp.int32)
    rep = lax.axis_index("rep").astype(jnp.int32)
    idx = jnp.stack([counts[0], shard])
    shard_bits = [1 << b for b in range(n.bit_length() - 1)]
    rep_bits = [1 << b for b in range(n_rep.bit_length() - 1)]

    def over_shard(x, bit):
        return swap(x, "shard", bit, n)

    def over_rep(x, bit):
        return swap(x, "rep", bit, n_rep)

    one_hot = (labels[:, None] == jnp.arange(class_table.shape[0], dtype=jnp.int32)[None, :])
    cond = dot(one_hot.astype(BF), class_table) + time_embed(timesteps, width)
    sig = jax.nn.sigmoid(cond)
    silu = (cond * sig).astype(BF)
    ada_rows = -(-ada_bias.shape[0] // width)
    hid_rows = hidden_bias.shape[0] // width
    group = jnp.concatenate(
        [
            silu,
            jnp.pad(ada_bias, (0, ada_rows * width - ada_bias.shape[0])).reshape(ada_rows, width),
            hidden_bias.reshape(hid_rows, width),
            jnp.stack([query_bias, value_bias, proj_bias, output_bias]).reshape(
                4 * part // width, width
            ),
        ],
        axis=0,
    )
    group = group[None]
    for bit in shard_bits:
        got = over_shard(group, bit)
        group = joined(bit_of(shard, bit), group, got)
    got = first_hop(qkv_weight, "shard", n)
    qkv_p = gather_xor(qkv_weight, got, "shard", n)
    group_silu = group[:, :slots].reshape(n * slots, n, part)
    at = slots
    ada_b = group[:, at : at + ada_rows].reshape(n, -1)[:, : ada_bias.shape[0]].reshape(1, -1)
    at += ada_rows
    hid_b = group[:, at : at + hid_rows].reshape(n * hid_rows, width).astype(F32)
    at += hid_rows
    qvpo = group[:, at:].reshape(n, 4, part).transpose(1, 0, 2).reshape(4, width).astype(F32)
    own_silu = lax.dynamic_index_in_dim(group_silu, shard, 1, keepdims=False)
    modulation = dot(own_silu, ada_weight).reshape(n, slots, -1)
    for bit in reversed(shard_bits):
        keep, send = halves(modulation, bit_of(shard, bit))
        got = over_shard(send, bit)
        modulation = keep + got
    mod = (modulation[0] + ada_b.astype(F32)).reshape(slots, 6, width)

    own_w = (hidden_weight, jnp.concatenate([output_weight, proj_weight], axis=0))
    got_w = []
    for i, weight in enumerate(own_w):
        got_w.append(first_hop(weight, "shard", n))

    rows = slots * seq
    steps = slots // LATENTS_PER_STEP if slots % LATENTS_PER_STEP == 0 else slots
    tok = (slots, seq, width)
    small = (slots, 8, width)
    dma = pltpu.SemaphoreType.DMA
    attn_in, qkv, probs, mixed = run(
        functools.partial(attn_fwd_kernel, n), steps, idx,
        (latents, mod), (qvpo,), tuple(qkv_p),
        [(tok, BF), ((slots, seq, 3 * width), BF), ((slots, HEADS, seq, seq), BF), (tok, BF)],
        [],
        [pltpu.VMEM((width, 3 * width), BF), dma((1, n))],
        2 * rows * width * 3 * width + 4 * rows * seq * width,
    )
    mixed, *got_w = lax.optimization_barrier((mixed, *got_w))
    hid_p, out_p = (gather_xor(own, got, "shard", n) for own, got in zip(own_w, got_w))
    align = 8 * n_rep
    out_end = output_weight.shape[0] * (width // LANES)
    hid_end = out_end + part * (hidden // LANES)
    proj_end = hid_end + part * (width // LANES)
    half = n // 2
    block_output, d_middle, d_mixed, small3, obias, hbias, pbias, keep, send = run(
        functools.partial(mlp_kernel, n), steps, idx,
        (latents, cotangent, mixed, mod), (qvpo, hid_b), (*hid_p, *out_p),
        [(tok, BF), (tok, F32), (tok, BF), (small, F32)],
        [((1, width), F32), ((1, hidden), F32), ((1, width), F32)]
        + [((half, round_up(proj_end, align), LANES), BF)] * 2,
        [pltpu.VMEM((width, hidden), BF), pltpu.VMEM((hidden, width), BF),
         pltpu.VMEM((width, width), BF), pltpu.VMEM((hidden, width), F32),
         pltpu.VMEM((width, hidden), F32), pltpu.VMEM((width, width), F32), dma((3, n))],
        12 * rows * width * hidden + 6 * rows * width * width,
    )

    for bit in shard_bits[:-1]:
        total = plus(keep, over_shard(send, bit))
        keep, send = total[0::2], total[1::2]
    got_mlp = over_shard(send, shard_bits[-1])
    n_sums = (hidden + 4 * width) // LANES
    qkv_end = part * 3 * width // LANES
    packed_qkv = round_up(qkv_end + n_sums, align)
    grad_input, riders, keep3, send3 = run(
        functools.partial(attn_bwd_kernel, n), steps, idx,
        (latents, d_middle, d_mixed, attn_in, qkv, probs, mod, small3),
        (silu.astype(F32), obias, hbias, pbias), tuple(qkv_p),
        [(tok, F32), ((slots * RIDER_ROWS, LANES), BF)],
        [((half, packed_qkv, LANES), BF)] * 2,
        [pltpu.VMEM((width, 3 * width), BF), pltpu.VMEM((width, 3 * width), F32),
         pltpu.VMEM((rows // steps, 3 * width), BF), pltpu.VMEM((1, width), F32),
         pltpu.VMEM((1, width), F32), pltpu.VMEM((RIDER_ROWS, LANES), F32),
         pltpu.VMEM((n_sums, LANES), F32), dma((1, n))],
        12 * rows * width * width + 8 * rows * seq * width,
    )

    def hop(x, move, bit):
        return move(x, bit)

    x = plus(keep, got_mlp)[0]
    k = 0
    for bit in rep_bits[:-1]:
        mine, out = halves(x, bit_of(rep, bit))
        got = hop(out, over_rep, bit)
        x = plus(mine, got)
        k += 1
    got = hop(x, over_rep, rep_bits[-1])
    x = plus(x, got)
    for bit in reversed(rep_bits[1:-1]):
        k += 1
        got = hop(x, over_rep, bit)
        x = joined(bit_of(rep, bit), x, got)
    got = hop(x, over_rep, rep_bits[0])
    side = jnp.stack([bit_of(rep, rep_bits[0]), shard])
    grad_out_w, grad_hid_w, grad_proj_w = finish(
        side, x, got,
        [(output_weight.shape[0], width), (part, hidden), (part, width)], None, n,
    )

    kept, out = keep3, send3
    k = 0
    for bit in shard_bits:
        got = hop(out, over_shard, bit)
        total = plus(kept, got)
        kept, out = total[0::2], total[1::2]
        k += 1
    mine, out = halves(kept[0], bit_of(rep, rep_bits[0]))
    got = hop(out, over_rep, rep_bits[0])
    x = plus(mine, got)
    for bit in rep_bits[1:]:
        k += 1
        got = hop(x, over_rep, bit)
        x = plus(x, got)
    got = hop(x, over_rep, rep_bits[0])
    grad_qkv_w, *bias_grads = finish(side, x, got, [(part, 3 * width)], (hidden, width), n)
    b_hid, b_q, b_v, b_p, b_o = (b.reshape(-1) for b in bias_grads)

    k = 0
    for move, bits in ((over_rep, rep_bits), (over_shard, shard_bits)):
        for bit in reversed(bits):
            got = hop(riders, move, bit)
            riders = jnp.concatenate([riders, got], axis=0)
            k += 1
    all_riders = riders.reshape(n * n_rep * slots, RIDER_ROWS * LANES)

    group_d_mod = all_riders.reshape(n, n_rep, slots, -1)[:, 0].reshape(n * slots, -1)
    partial_cond = dot_nt(group_d_mod[:, : 6 * width], ada_weight).reshape(n, slots, part)
    width_bits = len(shard_bits)
    held = {}
    for i in range(n):
        m = sum(((i >> b) & 1) << (width_bits - 1 - b) for b in range(width_bits))
        held[m] = {0: partial_cond[i]}
    for k, bit in enumerate(shard_bits):
        keys = [(m, src) for m in sorted(held) if m & bit for src in sorted(held[m])]
        packet = jnp.stack([held[m][src] for m, src in keys])
        packet = hop(packet, over_shard, bit)
        for i, (m, src) in enumerate(keys):
            held[m ^ bit][src ^ bit] = packet[i]
        held = {m: blocks_of for m, blocks_of in held.items() if not m & bit}
    stacked = jnp.stack([held[0][m] for m in range(n)])
    d_silu = jnp.concatenate(
        [lax.dynamic_index_in_dim(stacked, shard ^ j, 0, keepdims=False) for j in range(n)],
        axis=1,
    )
    grad_cond = d_silu * sig * (1.0 + cond * (1.0 - sig))

    all_d_mod = all_riders[:, : 6 * width]
    all_silu = lax.dynamic_index_in_dim(
        all_riders[:, 6 * width : 7 * width].reshape(-1, n, part), shard, 1, keepdims=False
    )
    grad_ada = dot_tn(all_silu, all_d_mod)
    grad_ada_b = dot(jnp.ones((8, all_d_mod.shape[0]), BF), all_d_mod)[0]

    def own(vector):
        return lax.dynamic_index_in_dim(vector.reshape(n, -1), shard, 0, keepdims=False)

    return (
        block_output,
        grad_input,
        grad_cond,
        grad_ada,
        own(grad_ada_b),
        grad_qkv_w,
        b_q,
        b_v,
        grad_proj_w,
        b_p,
        grad_hid_w,
        b_hid,
        grad_out_w,
        b_o,
    )


def solution(mesh):
    both = ("rep", "shard")
    in_specs = (
        P(both, None, None),
        P(both, None, None),
        P(both),
        P(both),
        P(both),
        P(),
        P("shard", None),
        P("shard"),
        P("shard", None),
        P("shard"),
        P("shard"),
        P("shard", None),
        P("shard"),
        P("shard", None),
        P("shard"),
        P("shard", None),
        P("shard"),
    )
    out_specs = (
        P(both, None, None),
        P(both, None, None),
        P(both, None),
        P("shard", None),
        P("shard"),
        P("shard", None),
        P("shard"),
        P("shard"),
        P("shard", None),
        P("shard"),
        P("shard", None),
        P("shard"),
        P("shard", None),
        P("shard"),
    )

    def body(*args):
        return per_device(mesh.shape["shard"], mesh.shape["rep"], *args)

    return jax.shard_map(
        body, mesh=mesh, in_specs=in_specs, out_specs=out_specs, check_vma=False
    )
```

```python
import functools
import math

import jax
import jax.numpy as jnp
from jax import lax
from jax.experimental import pallas as pl
from jax.experimental.pallas import tpu as pltpu
from jax.sharding import PartitionSpec as P


HEADS = 6
EPSILON = 1e-06
GELU_SCALE = math.sqrt(2.0 / math.pi)
GELU_CUBIC = 0.044715
LANES = 128
LATENTS_PER_STEP = 2
CHUNK = 512
RIDER_ROWS = 24
BF = jnp.bfloat16
F32 = jnp.float32
VMEM_LIMIT = 58 * 1024 * 1024


def dot(a, b):
    return jnp.dot(a, b, preferred_element_type=F32)


def dot_nt(a, b):
    return lax.dot_general(a, b, (((1,), (1,)), ((), ())), preferred_element_type=F32)


def dot_tn(a, b):
    return lax.dot_general(a, b, (((0,), (0,)), ((), ())), preferred_element_type=F32)


def row_mean(x):
    return jnp.mean(x, axis=-1, keepdims=True)


def layer_norm(x):
    centred = x - row_mean(x)
    inv = lax.rsqrt(row_mean(centred * centred) + EPSILON)
    return centred * inv, inv


def norm_backward(upstream, normed, inv):
    return inv * (upstream - row_mean(upstream) - normed * row_mean(upstream * normed))


def col_sum(x):
    return jnp.sum(x, axis=0, keepdims=True)


def load_pieces(idx_ref, pieces, whole, sems, first=0):
    rows = whole.shape[0] // len(pieces)
    copies = []
    for m, piece in enumerate(pieces):
        at = pl.multiple_of((idx_ref[1] ^ m) * rows, rows)
        source = piece.at[first : first + rows, :]
        copies.append(pltpu.make_async_copy(source, whole.at[pl.ds(at, rows), :], sems.at[m]))
    return copies


def store_blocks(ref, at, first, value):
    rows = value.shape[0]
    for j in range(value.shape[1] // LANES):
        ref[at, first : first + rows, :] = value[:, j * LANES : (j + 1) * LANES].astype(BF)
        first += rows
    return first


def store_rows(ref, first, value):
    for j in range(value.shape[1] // LANES):
        ref[first : first + 1, :] = value[:, j * LANES : (j + 1) * LANES]
        first += 1
    return first


def store_shares(idx_ref, n, keep, send, *totals, tail=None):
    for m in range(n):
        ref, at = (keep, send)[m % 2], m // 2
        first = 0
        for total in totals:
            rows = total.shape[0] // n
            start = pl.multiple_of((idx_ref[1] ^ m) * rows, rows)
            first = store_blocks(ref, at, first, total[pl.ds(start, rows), :])
        if tail is not None:
            ref[at, first : first + tail.shape[0], :] = tail[...].astype(BF)
            first += tail.shape[0]
        if first < ref.shape[1]:
            ref[at, first:, :] = jnp.zeros((ref.shape[1] - first, LANES), BF)


def attn_fwd_kernel(n, idx, lat, mod, qvpo, *rest):
    qkv_p = rest[:n]
    attn_in_o, qkv_o, probs_o, mixed_o, wqkv, sems = rest[n:]

    @pl.when(pl.program_id(0) == 0)
    def _():
        copies = load_pieces(idx, qkv_p, wqkv, sems.at[0])
        for c in copies:
            c.start()
        for c in copies:
            c.wait()

    group, seq, width = lat.shape
    rows = group * seq
    head = width // HEADS
    pair = 2 * head
    normed, _ = layer_norm(lat[...].astype(F32))
    attn_in = (normed * (1.0 + mod[:, 1:2, :]) + mod[:, 0:1, :]).astype(BF)
    attn_in_o[...] = attn_in
    attn_in = attn_in.reshape(rows, width)
    proj_all = dot(attn_in, wqkv[...])
    q = (proj_all[:, :width] + qvpo[0:1, :]).astype(BF)
    k = proj_all[:, width : 2 * width].astype(BF)
    v = (proj_all[:, 2 * width :] + qvpo[1:2, :]).astype(BF)
    qkv_o[:, :, :width] = q.reshape(group, seq, width)
    qkv_o[:, :, width : 2 * width] = k.reshape(group, seq, width)
    qkv_o[:, :, 2 * width :] = v.reshape(group, seq, width)
    low = lax.broadcasted_iota(jnp.int32, (seq, pair), 1) < head
    factor = head ** (-0.5)
    for g in range(group):
        here = slice(g * seq, (g + 1) * seq)
        for j in range(HEADS // 2):
            cols = slice(j * pair, (j + 1) * pair)
            qp, kp, vp = q[here, cols] * BF(factor), k[here, cols], v[here, cols]
            outs = []
            for h in range(2):
                mask = low if h == 0 else ~low
                s = dot_nt(kp, jnp.where(mask, qp, BF(0)))
                e = jnp.exp(s - jnp.max(s, axis=0, keepdims=True))
                p = (e * (1.0 / jnp.sum(e, axis=0, keepdims=True))).astype(BF)
                probs_o[g, 2 * j + h] = p
                outs.append(dot_tn(p, vp))
            mixed_o[g, :, cols] = jnp.where(low, outs[0], outs[1]).astype(BF)


def mlp_kernel(n, idx, lat, cot, mixed, mod, qvpo, hb, *rest):
    hid_p, out_p = rest[:n], rest[n : 2 * n]
    (
        block_o, dmid_o, dmix_o, small_o, obias_o, hbias_o, pbias_o, keep_o, send_o,
        whid, wout, wproj, acco, acch, accp, sems,
    ) = rest[2 * n :]
    step = pl.program_id(0)

    @pl.when(step == 0)
    def _():
        copies = (
            load_pieces(idx, hid_p, whid, sems.at[0])
            + load_pieces(idx, out_p, wout, sems.at[1])
            + load_pieces(idx, out_p, wproj, sems.at[2], first=wout.shape[0] // n)
        )
        for c in copies:
            c.start()
        for ref in (acco, acch, accp, obias_o, hbias_o, pbias_o):
            ref[...] = jnp.zeros_like(ref)
        for c in copies:
            c.wait()

    group, seq, width = lat.shape
    rows = group * seq

    def flat(x):
        return x.reshape(rows, width)

    def deep(x):
        return x.reshape(group, seq, width)

    slot = lax.broadcasted_iota(jnp.int32, (group, 1, 1), 0) + step * group
    live = jnp.where(slot < idx[0], 1.0, 0.0).astype(F32)
    gate1, shift2, scale2, gate2 = (mod[:, i : i + 1, :] for i in range(2, 6))
    mixed_v = flat(mixed[...])
    attn = deep(dot(mixed_v, wproj[...]) + qvpo[2:3, :])
    middle = lat[...].astype(F32) + gate1 * attn
    normed, inv = layer_norm(middle)
    mlp_in = flat((normed * (1.0 + scale2) + shift2).astype(BF))
    grad_out = live * cot[...].astype(F32)
    d_mlp = flat(grad_out * gate2)
    d_mlp_b = d_mlp.astype(BF)
    obias_o[...] += col_sum(d_mlp)
    mlp_out = qvpo[3:4, :] + jnp.zeros((rows, width), F32)
    d_mlp_in = jnp.zeros((rows, width), F32)
    hidden = whid.shape[1]
    chunk = CHUNK if hidden % CHUNK == 0 else width
    bias = jnp.concatenate([hb[j : j + 1, :] for j in range(hidden // width)], axis=1)
    for j in range(hidden // chunk):
        cols = slice(j * chunk, (j + 1) * chunk)
        u = dot(mlp_in, whid[:, cols]) + bias[:, cols]
        u2 = u * u
        t = jnp.tanh(u * (GELU_SCALE + (GELU_SCALE * GELU_CUBIC) * u2))
        half = 0.5 * (1.0 + t)
        slope = half + (0.5 * u) * (1.0 - t * t) * (
            GELU_SCALE + (3.0 * GELU_SCALE * GELU_CUBIC) * u2
        )
        act = (u * half).astype(BF)
        mlp_out += dot(act, wout[cols, :])
        acco[cols, :] += dot_tn(act, d_mlp_b)
        d_pre = dot_nt(d_mlp_b, wout[cols, :]) * slope
        hbias_o[:, cols] += col_sum(d_pre)
        d_pre_b = d_pre.astype(BF)
        acch[:, cols] += dot_tn(mlp_in, d_pre_b)
        d_mlp_in += dot_nt(d_pre_b, whid[:, cols])
    mlp_out = deep(mlp_out)
    d_mlp_in = deep(d_mlp_in)
    block_o[...] = (live * (middle + gate2 * mlp_out)).astype(BF)
    d_middle = grad_out + norm_backward(d_mlp_in * (1.0 + scale2), normed, inv)
    dmid_o[...] = d_middle
    d_attn = flat(d_middle * gate1)
    pbias_o[...] += col_sum(d_attn)
    d_attn_b = d_attn.astype(BF)
    accp[...] += dot_tn(mixed_v, d_attn_b)
    dmix_o[...] = deep(dot_nt(d_attn_b, wproj[...]).astype(BF))
    for g in range(group):
        small_o[g, 0:1] = col_sum(d_middle[g] * attn[g])
        small_o[g, 1:2] = col_sum(d_mlp_in[g])
        small_o[g, 2:3] = col_sum(d_mlp_in[g] * normed[g])
        small_o[g, 3:4] = col_sum(grad_out[g] * mlp_out[g])
        small_o[g, 4:8] = jnp.zeros((4, width), F32)

    @pl.when(step == pl.num_programs(0) - 1)
    def _():
        store_shares(idx, n, keep_o, send_o, acco, acch, accp)


def attn_bwd_kernel(
    n, idx, lat, dmid, dmix, attn_in, qkv, probs, mod, small, silu, obias, hbias, pbias, *rest
):
    qkv_p = rest[:n]
    (
        gin_o, riders_o, keep_o, send_o, wqkv, acc, dproj, qbias, vbias, lines, sums, sems,
    ) = rest[n:]
    step = pl.program_id(0)

    @pl.when(step == 0)
    def _():
        copies = load_pieces(idx, qkv_p, wqkv, sems.at[0])
        for c in copies:
            c.start()
        for c in copies:
            c.wait()
        acc[...] = jnp.zeros_like(acc)
        qbias[...] = jnp.zeros_like(qbias)
        vbias[...] = jnp.zeros_like(vbias)

    group, seq, width = lat.shape
    rows = group * seq
    head = width // HEADS
    pair = 2 * head
    factor = head ** (-0.5)
    low = lax.broadcasted_iota(jnp.int32, (seq, pair), 1) < head
    for g in range(group):
        here = slice(g * seq, (g + 1) * seq)
        for j in range(HEADS // 2):
            at = j * pair
            q = qkv[g, :, at : at + pair]
            k = qkv[g, :, width + at : width + at + pair]
            v = qkv[g, :, 2 * width + at : 2 * width + at + pair]
            dm = dmix[g, :, at : at + pair]
            parts = []
            for h in range(2):
                mask = low if h == 0 else ~low
                p_b = probs[g, 2 * j + h]
                p = p_b.astype(F32)
                dp = dot_nt(v, jnp.where(mask, dm, BF(0)))
                row_dot = jnp.sum(p * dp, axis=0, keepdims=True)
                ds = (p * (dp - row_dot) * factor).astype(BF)
                parts.append((dot_tn(ds, k), dot(ds, q), dot(p_b, dm)))
            dq, dk, dv = (jnp.where(low, a, b) for a, b in zip(*parts))
            qbias[:, at : at + pair] += col_sum(dq)
            vbias[:, at : at + pair] += col_sum(dv)
            dproj[here, at : at + pair] = dq.astype(BF)
            dproj[here, width + at : width + at + pair] = dk.astype(BF)
            dproj[here, 2 * width + at : 2 * width + at + pair] = dv.astype(BF)
    d_proj = dproj[...]
    d_attn_in = dot_nt(d_proj, wqkv[...]).reshape(group, seq, width)
    acc[...] += dot_tn(attn_in[...].reshape(rows, width), d_proj)
    normed, inv = layer_norm(lat[...].astype(F32))
    gin_o[...] = dmid[...] + norm_backward(d_attn_in * (1.0 + mod[:, 1:2, :]), normed, inv)
    for g in range(group):
        at = store_rows(lines, 0, col_sum(d_attn_in[g]))
        at = store_rows(lines, at, col_sum(d_attn_in[g] * normed[g]))
        for i in range(4):
            at = store_rows(lines, at, small[g, i : i + 1, :])
        at = store_rows(lines, at, silu[pl.ds(step * group + g, 1), :])
        lines[at:, :] = jnp.zeros((RIDER_ROWS - at, LANES), F32)
        riders_o[g * RIDER_ROWS : (g + 1) * RIDER_ROWS, :] = lines[...].astype(BF)

    @pl.when(step == pl.num_programs(0) - 1)
    def _():
        at = 0
        for value in (hbias, qbias, vbias, pbias, obias):
            at = store_rows(sums, at, value[...])
        store_shares(idx, n, keep_o, send_o, acc, tail=sums)


def per_step(shape, steps):
    rest = tuple(shape[1:])
    zeros = (0,) * len(rest)
    return pl.BlockSpec((shape[0] // steps,) + rest, lambda i, idx: (i,) + zeros)


def resident(shape):
    zeros = (0,) * len(shape)
    return pl.BlockSpec(tuple(shape), lambda i, idx: zeros)


def run(kernel, steps, idx, blocked, whole, pieces, outs_blocked, outs_whole, scratch, flops):
    out_shape = [jax.ShapeDtypeStruct(s, d) for s, d in outs_blocked + outs_whole]
    moved = sum(a.size * a.dtype.itemsize for a in list(blocked) + list(whole) + list(pieces))
    moved += sum(math.prod(s.shape) * s.dtype.itemsize for s in out_shape)
    return pl.pallas_call(
        kernel,
        out_shape=out_shape,
        grid_spec=pltpu.PrefetchScalarGridSpec(
            num_scalar_prefetch=1,
            grid=(steps,),
            in_specs=[per_step(a.shape, steps) for a in blocked]
            + [resident(a.shape) for a in whole]
            + [pl.BlockSpec(memory_space=pl.ANY) for _ in pieces],
            out_specs=[per_step(s, steps) for s, _ in outs_blocked]
            + [resident(s) for s, _ in outs_whole],
            scratch_shapes=scratch,
        ),
        compiler_params=pltpu.CompilerParams(
            dimension_semantics=("arbitrary",), vmem_limit_bytes=VMEM_LIMIT
        ),
        cost_estimate=pl.CostEstimate(flops=flops, transcendentals=0, bytes_accessed=moved),
    )(idx, *blocked, *whole, *pieces)


def finish_kernel(n, biases, side, x, got, *rest):
    outs, full = rest[:-1], rest[-1]
    half = x.shape[0]
    full[pl.ds(pl.multiple_of(side[0] * half, half), half), :] = x[...]
    full[pl.ds(pl.multiple_of((1 - side[0]) * half, half), half), :] = got[...]
    first = 0
    for out in outs if biases is None else outs[:1]:
        rows = out.shape[0]
        for j in range(out.shape[1] // LANES):
            out[:, j * LANES : (j + 1) * LANES] = full[first : first + rows, :].astype(F32)
            first += rows
    if biases is None:
        return
    hidden, width = biases
    lines = full[first : first + (hidden + 4 * width) // LANES, :].astype(F32)
    share = hidden // n // LANES
    for i in range(share):
        line = jnp.zeros((1, LANES), F32)
        for j in range(n):
            at = j * share + i
            line = jnp.where(side[1] == j, lines[at : at + 1, :], line)
        outs[1][i * LANES : (i + 1) * LANES] = line[0]
    part = width // n
    row = lax.broadcasted_iota(jnp.int32, (width, part), 0)
    col = lax.broadcasted_iota(jnp.int32, (width, part), 1)
    pick = jnp.where(row == col + side[1] * part, 1.0, 0.0).astype(BF)
    at = hidden // LANES
    for out in outs[2:]:
        vector = jnp.concatenate(
            [lines[at + i : at + i + 1, :] for i in range(width // LANES)], axis=1
        )
        wide = jnp.broadcast_to(vector, (8, width)).astype(BF)
        out[...] = dot(wide, pick)[0:1, :]
        at += width // LANES


def finish(side, x, got, shapes, biases, n):
    shapes = list(shapes)
    if biases is not None:
        shapes += [(biases[0] // n,)] + [(1, biases[1] // n)] * 4
    spec = pl.BlockSpec(memory_space=pltpu.VMEM)
    return pl.pallas_call(
        functools.partial(finish_kernel, n, biases),
        out_shape=[jax.ShapeDtypeStruct(shape, F32) for shape in shapes],
        in_specs=[pl.BlockSpec(memory_space=pltpu.SMEM), spec, spec],
        out_specs=[spec] * len(shapes),
        scratch_shapes=[pltpu.VMEM((2 * x.shape[0], LANES), BF)],
        cost_estimate=pl.CostEstimate(
            flops=0, transcendentals=0, bytes_accessed=12 * x.size
        ),
    )(side, x, got)


def finish_ada_kernel(side, riders, ada, weight_o, bias_o, cond_o):
    part, wide = ada.shape
    width = wide // 6
    d_mod = riders[:, :wide]
    row = lax.broadcasted_iota(jnp.int32, (width, part), 0)
    col = lax.broadcasted_iota(jnp.int32, (width, part), 1)
    pick = jnp.where(row == col + side[1] * part, 1.0, 0.0).astype(BF)
    silu = dot(riders[:, wide : wide + width], pick).astype(BF)
    weight_o[...] = dot_tn(silu, d_mod)
    bias_o[...] = dot(jnp.ones((8, riders.shape[0]), BF), d_mod)[0]
    cond_o[...] = dot_nt(d_mod, ada[...])


def finish_ada(side, riders, ada):
    part, wide = ada.shape
    spec = pl.BlockSpec(memory_space=pltpu.VMEM)
    return pl.pallas_call(
        finish_ada_kernel,
        name="finish_ada",
        out_shape=[
            jax.ShapeDtypeStruct((part, wide), F32),
            jax.ShapeDtypeStruct((wide,), F32),
            jax.ShapeDtypeStruct((riders.shape[0], part), F32),
        ],
        in_specs=[pl.BlockSpec(memory_space=pltpu.SMEM), spec, spec],
        out_specs=[spec] * 3,
        cost_estimate=pl.CostEstimate(
            flops=4 * riders.shape[0] * part * wide, transcendentals=0,
            bytes_accessed=2 * riders.size + 6 * part * wide,
        ),
    )(side, riders, ada)


def time_embed(step_ids, model_width):
    half_width = model_width // 2
    frequency = jnp.exp(-math.log(10000.0) * jnp.arange(half_width, dtype=F32) / half_width)
    angles = step_ids.astype(F32)[:, None] * frequency[None, :]
    return jnp.concatenate([jnp.cos(angles), jnp.sin(angles)], axis=1)


def swap(x, axis, mask, size):
    return lax.ppermute(x, axis, [(i, i ^ mask) for i in range(size)])


def first_hop(own, axis, size):
    return swap(own, axis, size // 2, size)


def gather_xor(own, got, axis, size):
    bit = size // 2
    pieces = {0: own, bit: got}
    bit //= 2
    while bit:
        for m in list(pieces):
            pieces[m ^ bit] = swap(pieces[m], axis, bit, size)
        bit //= 2
    return [pieces[m] for m in range(size)]


def bit_of(index, bit):
    return (index // bit) % 2


def joined(mine, x, got):
    first = jnp.where(mine == 0, x, got)
    second = jnp.where(mine == 0, got, x)
    return jnp.concatenate([first, second], axis=0)


def halves(x, mine):
    x = x.reshape((2, x.shape[0] // 2) + x.shape[1:])
    keep = lax.dynamic_index_in_dim(x, mine, 0, keepdims=False)
    send = lax.dynamic_index_in_dim(x, 1 - mine, 0, keepdims=False)
    return keep, send


def plus(a, b):
    return (a.astype(F32) + b.astype(F32)).astype(BF)


def round_up(value, step):
    return -(-value // step) * step


def per_device(
    n_shard,
    n_rep,
    latents,
    cotangent,
    counts,
    labels,
    timesteps,
    class_table,
    ada_weight,
    ada_bias,
    qkv_weight,
    query_bias,
    value_bias,
    proj_weight,
    proj_bias,
    hidden_weight,
    hidden_bias,
    output_weight,
    output_bias,
):
    n = n_shard
    slots, seq, width = latents.shape
    hidden = hidden_weight.shape[1]
    part = width // n
    shard = lax.axis_index("shard").astype(jnp.int32)
    rep = lax.axis_index("rep").astype(jnp.int32)
    idx = jnp.stack([counts[0], shard])
    shard_bits = [1 << b for b in range(n.bit_length() - 1)]
    rep_bits = [1 << b for b in range(n_rep.bit_length() - 1)]

    def over_shard(x, bit):
        return swap(x, "shard", bit, n)

    def over_rep(x, bit):
        return swap(x, "rep", bit, n_rep)

    one_hot = (labels[:, None] == jnp.arange(class_table.shape[0], dtype=jnp.int32)[None, :])
    cond = dot(one_hot.astype(BF), class_table) + time_embed(timesteps, width)
    sig = jax.nn.sigmoid(cond)
    silu = (cond * sig).astype(BF)
    ada_rows = -(-ada_bias.shape[0] // width)
    hid_rows = hidden_bias.shape[0] // width
    group = jnp.concatenate(
        [
            silu,
            jnp.pad(ada_bias, (0, ada_rows * width - ada_bias.shape[0])).reshape(ada_rows, width),
            hidden_bias.reshape(hid_rows, width),
            jnp.stack([query_bias, value_bias, proj_bias, output_bias]).reshape(
                4 * part // width, width
            ),
        ],
        axis=0,
    )
    group = group[None]
    for bit in shard_bits:
        got = over_shard(group, bit)
        group = joined(bit_of(shard, bit), group, got)
    got = first_hop(qkv_weight, "shard", n)
    qkv_p = gather_xor(qkv_weight, got, "shard", n)
    group_silu = group[:, :slots].reshape(n * slots, n, part)
    at = slots
    ada_b = group[:, at : at + ada_rows].reshape(n, -1)[:, : ada_bias.shape[0]].reshape(1, -1)
    at += ada_rows
    hid_b = group[:, at : at + hid_rows].reshape(n * hid_rows, width).astype(F32)
    at += hid_rows
    qvpo = group[:, at:].reshape(n, 4, part).transpose(1, 0, 2).reshape(4, width).astype(F32)
    own_silu = lax.dynamic_index_in_dim(group_silu, shard, 1, keepdims=False)
    modulation = dot(own_silu, ada_weight).reshape(n, slots, -1)
    for bit in reversed(shard_bits):
        keep, send = halves(modulation, bit_of(shard, bit))
        got = over_shard(send, bit)
        modulation = keep + got
    mod = (modulation[0] + ada_b.astype(F32)).reshape(slots, 6, width)

    own_w = (hidden_weight, jnp.concatenate([output_weight, proj_weight], axis=0))
    got_w = []
    for i, weight in enumerate(own_w):
        got_w.append(first_hop(weight, "shard", n))

    rows = slots * seq
    steps = slots // LATENTS_PER_STEP if slots % LATENTS_PER_STEP == 0 else slots
    tok = (slots, seq, width)
    small = (slots, 8, width)
    dma = pltpu.SemaphoreType.DMA
    attn_in, qkv, probs, mixed = run(
        functools.partial(attn_fwd_kernel, n), steps, idx,
        (latents, mod), (qvpo,), tuple(qkv_p),
        [(tok, BF), ((slots, seq, 3 * width), BF), ((slots, HEADS, seq, seq), BF), (tok, BF)],
        [],
        [pltpu.VMEM((width, 3 * width), BF), dma((1, n))],
        2 * rows * width * 3 * width + 4 * rows * seq * width,
    )
    mixed, *got_w = lax.optimization_barrier((mixed, *got_w))
    hid_p, out_p = (gather_xor(own, got, "shard", n) for own, got in zip(own_w, got_w))
    align = 8 * n_rep
    out_end = output_weight.shape[0] * (width // LANES)
    hid_end = out_end + part * (hidden // LANES)
    proj_end = hid_end + part * (width // LANES)
    half = n // 2
    block_output, d_middle, d_mixed, small3, obias, hbias, pbias, keep, send = run(
        functools.partial(mlp_kernel, n), steps, idx,
        (latents, cotangent, mixed, mod), (qvpo, hid_b), (*hid_p, *out_p),
        [(tok, BF), (tok, F32), (tok, BF), (small, F32)],
        [((1, width), F32), ((1, hidden), F32), ((1, width), F32)]
        + [((half, round_up(proj_end, align), LANES), BF)] * 2,
        [pltpu.VMEM((width, hidden), BF), pltpu.VMEM((hidden, width), BF),
         pltpu.VMEM((width, width), BF), pltpu.VMEM((hidden, width), F32),
         pltpu.VMEM((width, hidden), F32), pltpu.VMEM((width, width), F32), dma((3, n))],
        12 * rows * width * hidden + 6 * rows * width * width,
    )

    for bit in shard_bits[:-1]:
        total = plus(keep, over_shard(send, bit))
        keep, send = total[0::2], total[1::2]
    got_mlp = over_shard(send, shard_bits[-1])
    n_sums = (hidden + 4 * width) // LANES
    qkv_end = part * 3 * width // LANES
    packed_qkv = round_up(qkv_end + n_sums, align)
    grad_input, riders, keep3, send3 = run(
        functools.partial(attn_bwd_kernel, n), steps, idx,
        (latents, d_middle, d_mixed, attn_in, qkv, probs, mod, small3),
        (silu.astype(F32), obias, hbias, pbias), tuple(qkv_p),
        [(tok, F32), ((slots * RIDER_ROWS, LANES), BF)],
        [((half, packed_qkv, LANES), BF)] * 2,
        [pltpu.VMEM((width, 3 * width), BF), pltpu.VMEM((width, 3 * width), F32),
         pltpu.VMEM((rows // steps, 3 * width), BF), pltpu.VMEM((1, width), F32),
         pltpu.VMEM((1, width), F32), pltpu.VMEM((RIDER_ROWS, LANES), F32),
         pltpu.VMEM((n_sums, LANES), F32), dma((1, n))],
        12 * rows * width * width + 8 * rows * seq * width,
    )

    def hop(x, move, bit):
        return move(x, bit)

    x = plus(keep, got_mlp)[0]
    k = 0
    for bit in rep_bits[:-1]:
        mine, out = halves(x, bit_of(rep, bit))
        got = hop(out, over_rep, bit)
        x = plus(mine, got)
        k += 1
    got = hop(x, over_rep, rep_bits[-1])
    x = plus(x, got)
    for bit in reversed(rep_bits[1:-1]):
        k += 1
        got = hop(x, over_rep, bit)
        x = joined(bit_of(rep, bit), x, got)
    got = hop(x, over_rep, rep_bits[0])
    side = jnp.stack([bit_of(rep, rep_bits[0]), shard])
    grad_out_w, grad_hid_w, grad_proj_w = finish(
        side, x, got,
        [(output_weight.shape[0], width), (part, hidden), (part, width)], None, n,
    )

    kept, out = keep3, send3
    k = 0
    for bit in shard_bits:
        got = hop(out, over_shard, bit)
        total = plus(kept, got)
        kept, out = total[0::2], total[1::2]
        k += 1
    mine, out = halves(kept[0], bit_of(rep, rep_bits[0]))
    got = hop(out, over_rep, rep_bits[0])
    x = plus(mine, got)
    for bit in rep_bits[1:]:
        k += 1
        got = hop(x, over_rep, bit)
        x = plus(x, got)
    got = hop(x, over_rep, rep_bits[0])
    grad_qkv_w, *bias_grads = finish(side, x, got, [(part, 3 * width)], (hidden, width), n)
    b_hid, b_q, b_v, b_p, b_o = (b.reshape(-1) for b in bias_grads)

    k = 0
    for move, bits in ((over_rep, rep_bits), (over_shard, shard_bits)):
        for bit in reversed(bits):
            got = hop(riders, move, bit)
            riders = jnp.concatenate([riders, got], axis=0)
            k += 1
    all_riders = riders.reshape(n * n_rep * slots, RIDER_ROWS * LANES)

    grad_ada, grad_ada_b, all_cond = finish_ada(side, all_riders, ada_weight)
    partial_cond = all_cond.reshape(n, n_rep, slots, part)[:, 0]
    width_bits = len(shard_bits)
    held = {}
    for i in range(n):
        m = sum(((i >> b) & 1) << (width_bits - 1 - b) for b in range(width_bits))
        held[m] = {0: partial_cond[i]}
    for k, bit in enumerate(shard_bits):
        keys = [(m, src) for m in sorted(held) if m & bit for src in sorted(held[m])]
        packet = jnp.stack([held[m][src] for m, src in keys])
        packet = hop(packet, over_shard, bit)
        for i, (m, src) in enumerate(keys):
            held[m ^ bit][src ^ bit] = packet[i]
        held = {m: blocks_of for m, blocks_of in held.items() if not m & bit}
    stacked = jnp.stack([held[0][m] for m in range(n)])
    d_silu = jnp.concatenate(
        [lax.dynamic_index_in_dim(stacked, shard ^ j, 0, keepdims=False) for j in range(n)],
        axis=1,
    )
    grad_cond = d_silu * sig * (1.0 + cond * (1.0 - sig))

    def own(vector):
        return lax.dynamic_index_in_dim(vector.reshape(n, -1), shard, 0, keepdims=False)

    return (
        block_output,
        grad_input,
        grad_cond,
        grad_ada,
        own(grad_ada_b),
        grad_qkv_w,
        b_q,
        b_v,
        grad_proj_w,
        b_p,
        grad_hid_w,
        b_hid,
        grad_out_w,
        b_o,
    )


def solution(mesh):
    both = ("rep", "shard")
    in_specs = (
        P(both, None, None),
        P(both, None, None),
        P(both),
        P(both),
        P(both),
        P(),
        P("shard", None),
        P("shard"),
        P("shard", None),
        P("shard"),
        P("shard"),
        P("shard", None),
        P("shard"),
        P("shard", None),
        P("shard"),
        P("shard", None),
        P("shard"),
    )
    out_specs = (
        P(both, None, None),
        P(both, None, None),
        P(both, None),
        P("shard", None),
        P("shard"),
        P("shard", None),
        P("shard"),
        P("shard"),
        P("shard", None),
        P("shard"),
        P("shard", None),
        P("shard"),
        P("shard", None),
        P("shard"),
    )

    def body(*args):
        return per_device(mesh.shape["shard"], mesh.shape["rep"], *args)

    return jax.shard_map(
        body, mesh=mesh, in_specs=in_specs, out_specs=out_specs, check_vma=False
    )
```
